32 devices in a mesh: row: 8 (over z, y), col: 4 (over x, core).
Axes of the slice: x: 2, y: 2, z: 4, core: 2. Of those that a mesh axis runs over, the one named last changes fastest.
Arguments:
- current_image: float32 [16, 1024, 1024], P(None, 'row', 'col'), may hold values from -6 to 6
- measured: float32 [16, 8, 16, 128], P('col', 'row'), may hold values from -6 to 6
- ray_weight: float32 [16, 8, 128], P('col', 'row'), may hold values from 0.25 to 4
- angle_ids: int32 [16], replicated, may hold values from 0 to 255, as said below
- shadow_start: int32 [8, 8, 16], replicated, may hold values from 0 to 896, as said below
Outputs:
- smoothed_image: float32 [16, 1024, 1024], P(None, 'row', 'col')
The draws below stay inside these ranges and needn't reach their ends.
Inputs may be any that keep to these rules, and one draw needn't show every extreme that they name: `angle_ids`: distinct angle numbers. `shadow_start`: the shadow of a tile covers the 128 detector bins from this bin on, so it touches one or two detector blocks.
All inputs are finite; a program needn't handle non-finite values.
Results may differ from the reference program's by a relative error of at most 0.0033.
Values may be sent and summed in bfloat16 or wider, within the bound.
A program may use at most 64 MiB of HBM per device.

```python
import math
import jax
import jax.numpy as jnp
from jax import lax

TILE = 128
SLICES = 16
ANGLES = 16
ALL_ANGLES = 256
TV_STEPS = 4
SIDE_TILES = 8
IMG = 1024
BLOCKS = 8
DET = 1024
N_ROW = 8


def angle_helper(key):
    stride = ALL_ANGLES // ANGLES
    offset = jax.random.randint(jax.random.fold_in(key, 11), (), 0, stride)
    return (offset + stride * jnp.arange(ANGLES, dtype=jnp.int32)).astype(jnp.int32)


def draw_angle_ids(key, part):
    return angle_helper(key)


def draw_shadow_start(key, part):
    total = SIDE_TILES * SIDE_TILES * ANGLES
    starts = jax.random.randint(jax.random.fold_in(key, 23), (total,), 0, DET - TILE + 1)
    places = jax.random.permutation(jax.random.fold_in(key, 29), total)
    starts = starts.at[places[0]].set(0)
    starts = starts.at[places[1]].set(DET - TILE)
    return starts.reshape(SIDE_TILES, SIDE_TILES, ANGLES).astype(jnp.int32)


def shard_levels(own_key, extent, pieces, low, high):
    factor_of, own = 1.0, jax.random.fold_in(own_key, 6)
    for axis_at, blocks in pieces:
        draws = jnp.exp(jax.random.uniform(jax.random.fold_in(own, axis_at), (blocks,), jnp.float32, low / len(pieces), high / len(pieces)))
        factor_of = factor_of * jnp.repeat(draws, extent[axis_at] // blocks).reshape([-1 if axis == axis_at else 1 for axis in range(len(extent))])
    return factor_of


def bell_draw(own_key, extent, scale, limit, split=(), held_as=jnp.bfloat16):
    values = scale * jax.random.normal(own_key, extent, jnp.float32)
    if split:
        values = values * shard_levels(own_key, extent, split, -0.22, 0.18)
    return jnp.clip(values, -limit, limit).astype(held_as)


def setup_inputs(seed: int = 0) -> dict:
    arg_keys = jax.random.split(jax.random.key(seed), 6)
    return {
        "current_image": bell_draw(arg_keys[0], (SLICES, IMG, IMG), 1.0, 6.0, ((1, 8), (2, 4)), jnp.float32),
        "measured": bell_draw(arg_keys[1], (ANGLES, BLOCKS, SLICES, TILE), 1.0, 6.0, ((0, 4), (1, 8)), jnp.float32),
        "ray_weight": jnp.clip(jnp.exp(math.log(4.0) - 2.7725887 * jax.random.uniform(arg_keys[2], (ANGLES, BLOCKS, TILE), jnp.float32) ** shard_levels(arg_keys[2], (ANGLES, BLOCKS, TILE), ((0, 4), (1, 8)), -0.2, 0.2)), 0.25, 4.0),
        "angle_ids": draw_angle_ids(jax.random.fold_in(arg_keys[5], 71), 0),
        "shadow_start": draw_shadow_start(jax.random.fold_in(arg_keys[5], 71), 0),
    }


inverse_root = 0.7071067811865476
proj_scale = 0.03125
relaxation = 8.0
smoothing = 0.25
descent_step = 0.05

def tile_weights(angle_number):
    radians = angle_number.astype(jnp.float32) * (math.pi / ALL_ANGLES)
    cosine = jnp.cos(radians)
    sine_value = jnp.sin(radians)
    centre = (TILE - 1) / 2.0
    position = jnp.arange(TILE, dtype=jnp.float32) - centre
    along_bins = TILE / 2.0 + (position[:, None] * cosine + position[None, :] * sine_value) * inverse_root
    centres = jnp.arange(TILE, dtype=jnp.float32) + 0.5
    hat_values = jnp.maximum(0.0, 1.0 - jnp.abs(along_bins.reshape(-1, 1) - centres[None, :]))
    return (hat_values * proj_scale).astype(jnp.bfloat16)

def ramp(offset):
    is_odd = offset % 2 != 0
    nonzero = jnp.where(offset == 0, 1, offset).astype(jnp.float32)
    values = jnp.where(is_odd, -1.0 / (math.pi * math.pi * nonzero * nonzero), 0.0)
    values = jnp.where(offset == 0, 0.25, values)
    return jnp.where(jnp.abs(offset) < TILE, values, 0.0).astype(jnp.float32)

def tv_gradient(padded):
    corner = padded[:, :-1, :-1]
    step_down = padded[:, 1:, :-1] - corner
    step_right = padded[:, :-1, 1:] - corner
    magnitude = jnp.sqrt(smoothing * smoothing + step_down * step_down + step_right * step_right)
    flow_down = step_down / magnitude
    flow_right = step_right / magnitude
    return flow_down[:, :-1, 1:] - flow_down[:, 1:, 1:] + flow_right[:, 1:, :-1] - flow_right[:, 1:, 1:]

def reference(current_image, measured, ray_weight, angle_ids, shadow_start):
    count = N_ROW * N_ROW
    tile_data = current_image.reshape(SLICES, N_ROW, TILE, N_ROW, TILE).transpose(1, 3, 0, 2, 4)
    tile_data = tile_data.reshape(count * SLICES, TILE * TILE).astype(jnp.bfloat16).astype(jnp.float32)
    starts = shadow_start.reshape(count, ANGLES)
    offsets = jnp.arange(TILE, dtype=jnp.int32)

    def project(angle_index):
        weights = tile_weights(angle_ids[angle_index]).astype(jnp.float32)
        partial_value = jnp.dot(tile_data, weights, precision=lax.Precision.HIGHEST)
        partial_value = partial_value.reshape(count, SLICES, TILE).transpose(1, 0, 2).reshape(SLICES, count * TILE)
        bin_index = (starts[:, angle_index][:, None] + offsets[None, :]).reshape(-1)
        return jnp.zeros((SLICES, DET), jnp.float32).at[:, bin_index].add(partial_value)
    ray_sums = lax.map(project, jnp.arange(ANGLES, dtype=jnp.int32))
    natural = measured.transpose(0, 2, 1, 3).reshape(ANGLES, SLICES, DET)
    weight_rows = ray_weight.reshape(ANGLES, 1, DET)
    residual = weight_rows * (natural - ray_sums)
    detector = jnp.arange(DET, dtype=jnp.int32)
    ramp_table = ramp(detector[None, :] - detector[:, None])
    filtered = jnp.einsum('asi,ij->asj', residual, ramp_table, precision=lax.Precision.HIGHEST)
    filtered = filtered.astype(jnp.bfloat16).astype(jnp.float32)

    def accumulate(angle_index, running):
        weights = tile_weights(angle_ids[angle_index]).astype(jnp.float32)
        bin_index = starts[:, angle_index][:, None] + offsets[None, :]
        shadow = filtered[angle_index][:, bin_index]
        shadow = shadow.transpose(1, 0, 2).reshape(count * SLICES, TILE)
        return running + jnp.dot(shadow, weights.T, precision=lax.Precision.HIGHEST)
    update = lax.fori_loop(0, ANGLES, accumulate, jnp.zeros((count * SLICES, TILE * TILE), jnp.float32))
    update = update.reshape(N_ROW, N_ROW, SLICES, TILE, TILE).transpose(2, 0, 3, 1, 4).reshape(SLICES, IMG, IMG)
    current = current_image + relaxation * update
    for repeat in range(TV_STEPS):
        padded = jnp.pad(current, ((0, 0), (1, 1), (1, 1)))
        current = current - descent_step * tv_gradient(padded)
    return current
```

```python
import math

import jax
import jax.numpy as jnp
from jax import lax
from jax.experimental import pallas as pl
from jax.experimental.pallas import tpu as pltpu
from jax.sharding import PartitionSpec as P

TILE = 128
ANGLES = 16
ALL_ANGLES = 256
TV_STEPS = 4


inverse_root = 0.7071067811865476
proj_scale = 0.03125
relaxation = 8.0
smoothing = 0.25
descent_step = 0.05


def with_halo(value, sides, width):
    for axis, dim in sides:
        peers, length = (lax.axis_size(axis), value.shape[dim])
        up = [(i, (i + 1) % peers) for i in range(peers - 1)]
        down = [(j, i) for i, j in up]
        last = lax.slice_in_dim(value, length - width, length, axis=dim)
        initial = lax.slice_in_dim(value, 0, width, axis=dim)
        before = lax.ppermute(last, axis, up)
        after = lax.ppermute(initial, axis, down)
        value = jnp.concatenate([before, value, after], axis=dim)
    return value


def angle_table(angle_ids):
    radians = angle_ids.astype(jnp.float32) * (math.pi / ALL_ANGLES)
    row_step = jnp.cos(radians) * inverse_root
    col_step = jnp.sin(radians) * inverse_root
    steep = jnp.where(jnp.abs(col_step) >= jnp.abs(row_step), 0, 1).astype(jnp.int32)
    return row_step, col_step, steep


def lookup(table, index):
    return jnp.take_along_axis(table, index, axis=1, mode="promise_in_bounds")


def pieces(slices, across):
    return [(t, g) for t in range(across) for g in range(slices // 8)]


LINES = 8


def forward_kernel(slow_ref, fast_ref, steep_ref, x_ref, out_ref):
    slices = x_ref.shape[2]
    across = x_ref.shape[3] // TILE
    parts = pieces(slices, across)
    centre = (TILE - 1) / 2.0
    lanes = lax.broadcasted_iota(jnp.int32, (8, TILE), 1).astype(jnp.float32)

    def one_angle(a, carry):
        slow = slow_ref[a]
        fast = fast_ref[a]
        steep = steep_ref[a]
        inverse = 1.0 / jnp.full((8, TILE), fast, jnp.float32)
        b = jnp.abs(jnp.full((8, TILE), fast, jnp.float32))
        one_b = 1.0 - b
        two_b = 1.0 - 2.0 * b
        base = (lanes + (0.5 - TILE / 2.0)) * inverse + centre
        tilt = slow * inverse

        def some_lines(block, sums):
            sums = list(sums)
            for k in range(LINES):
                line = block * LINES + k
                q = base - (line.astype(jnp.float32) - centre) * tilt
                whole = jnp.floor(q)
                t = b * (q - whole)
                first = whole.astype(jnp.int32) - 1
                weights = (
                    jnp.maximum(one_b - t, 0.0),
                    1.0 - t,
                    one_b + t,
                    jnp.maximum(two_b + t, 0.0),
                )
                picks = []
                for j, w in enumerate(weights):
                    at = first + j
                    index = at & (TILE - 1)
                    picks.append((index, jnp.where(index == at, w, 0.0)))
                for n, (tile, group) in enumerate(parts):
                    row = x_ref[
                        steep, line, group * 8 : group * 8 + 8, tile * TILE : (tile + 1) * TILE
                    ]
                    (i0, w0), (i1, w1), (i2, w2), (i3, w3) = picks
                    sums[n] = sums[n] + (
                        (lookup(row, i0) * w0 + lookup(row, i1) * w1)
                        + (lookup(row, i2) * w2 + lookup(row, i3) * w3)
                    )
            return tuple(sums)

        zero = jnp.zeros((8, TILE), jnp.float32)
        sums = lax.fori_loop(0, TILE // LINES, some_lines, (zero,) * len(parts))
        for n, (tile, group) in enumerate(parts):
            out_ref[a, tile, group * 8 : group * 8 + 8, :] = sums[n] * proj_scale
        return carry

    lax.fori_loop(0, slow_ref.shape[0], one_angle, jnp.int32(0))


def project(lines, table):
    row_step, col_step, steep = table
    slow = jnp.where(steep == 0, row_step, col_step)
    fast = jnp.where(steep == 0, col_step, row_step)
    slices = lines.shape[2]
    across = lines.shape[3] // TILE
    smem = pl.BlockSpec(memory_space=pltpu.SMEM)
    vmem = pl.BlockSpec(memory_space=pltpu.VMEM)
    return pl.pallas_call(
        forward_kernel,
        out_shape=jax.ShapeDtypeStruct((ANGLES, across, slices, TILE), jnp.float32),
        in_specs=[smem, smem, smem, vmem],
        out_specs=vmem,
        name="project",
    )(slow, fast, steep, lines)


def backward_kernel(row_ref, col_ref, shadow_ref, x_ref, out_ref, value_ref, step_ref, base_ref):
    slices = x_ref.shape[1]
    across = x_ref.shape[2] // TILE
    angles = shadow_ref.shape[0]
    parts = pieces(slices, across)
    centre = (TILE - 1) / 2.0
    lanes = lax.broadcasted_iota(jnp.int32, (8, TILE), 1).astype(jnp.float32) - centre
    scale = relaxation * proj_scale
    for a in range(angles):
        base_ref[a] = TILE / 2.0 - 0.5 + lanes * col_ref[a]
        for n, (tile, group) in enumerate(parts):
            value = shadow_ref[a, tile, group * 8 : group * 8 + 8, :].astype(jnp.float32) * scale
            value_ref[a, n] = value
            step_ref[a, n] = jnp.roll(value, -1, axis=1) - value

    def one_row(u, carry):
        place = u.astype(jnp.float32) - centre
        sums = [
            x_ref[u, g * 8 : g * 8 + 8, t * TILE : (t + 1) * TILE].astype(jnp.float32)
            for t, g in parts
        ]
        for a in range(angles):
            z = base_ref[a] + place * row_ref[a]
            z = jnp.minimum(jnp.maximum(z, 0.0), TILE - 1.00001)
            whole = jnp.floor(z)
            part = z - whole
            index = whole.astype(jnp.int32)
            for n in range(len(parts)):
                sums[n] = sums[n] + (
                    lookup(value_ref[a, n], index) + part * lookup(step_ref[a, n], index)
                )
        for n, (t, g) in enumerate(parts):
            out_ref[u, g * 8 : g * 8 + 8, t * TILE : (t + 1) * TILE] = sums[n]
        return carry

    lax.fori_loop(0, TILE, one_row, jnp.int32(0))


def back_project(shadows, rows, table):
    row_step, col_step, steep = table
    angles, across, slices, unused = shadows.shape
    smem = pl.BlockSpec(memory_space=pltpu.SMEM)
    vmem = pl.BlockSpec(memory_space=pltpu.VMEM)
    parts = across * slices // 8
    return pl.pallas_call(
        backward_kernel,
        out_shape=jax.ShapeDtypeStruct(rows.shape, jnp.float32),
        in_specs=[smem, smem, vmem, vmem],
        out_specs=vmem,
        scratch_shapes=[
            pltpu.VMEM((angles, parts, 8, TILE), jnp.float32),
            pltpu.VMEM((angles, parts, 8, TILE), jnp.float32),
            pltpu.VMEM((angles, 8, TILE), jnp.float32),
        ],
        name="back_project",
    )(row_step, col_step, shadows, rows)


def ramp(offset):
    is_odd = offset % 2 != 0
    nonzero = jnp.where(offset == 0, 1, offset).astype(jnp.float32)
    values = jnp.where(is_odd, -1.0 / (math.pi * math.pi * nonzero * nonzero), 0.0)
    values = jnp.where(offset == 0, 0.25, values)
    return jnp.where(jnp.abs(offset) < TILE, values, 0.0)


def tv_gradient(padded):
    corner = padded[:, :-1, :-1]
    step_down = padded[:, 1:, :-1] - corner
    step_right = padded[:, :-1, 1:] - corner
    magnitude = jnp.sqrt(smoothing * smoothing + step_down * step_down + step_right * step_right)
    flow_down = step_down / magnitude
    flow_right = step_right / magnitude
    return (
        flow_down[:, :-1, 1:]
        - flow_down[:, 1:, 1:]
        + flow_right[:, 1:, :-1]
        - flow_right[:, 1:, 1:]
    )


def selector(offsets, kind):
    wide = jnp.arange(2 * TILE, dtype=jnp.int32)
    narrow = jnp.arange(TILE, dtype=jnp.int32)
    return (
        wide[None, :, None] == offsets.reshape(-1)[:, None, None] + narrow[None, None, :]
    ).astype(kind)


def place(partial_value, offsets):
    chooser = selector(offsets, jnp.float32)
    return jnp.einsum(
        "bsm,bkm->bsk",
        partial_value,
        chooser,
        precision=lax.Precision.HIGHEST,
        preferred_element_type=jnp.float32,
    )


def window(two_blocks, offsets):
    leading = offsets.shape
    inner = two_blocks.shape[len(leading) :]
    flat = two_blocks.reshape((-1,) + inner)
    chooser = selector(offsets, jnp.bfloat16)
    picked = jnp.einsum("bsk,bkm->bsm", flat, chooser, preferred_element_type=jnp.float32)
    return picked.astype(jnp.bfloat16).reshape(leading + inner[:-1] + (TILE,))


def pick_rows(table, first_rows, second_rows):
    leading = first_rows.shape
    total = table.shape[0]
    indices = jnp.stack([first_rows, second_rows], axis=-1).reshape(-1)
    onehot = (indices[:, None] == jnp.arange(total, dtype=jnp.int32)[None, :]).astype(jnp.bfloat16)
    picked = jnp.dot(onehot, table.reshape(total, -1), preferred_element_type=jnp.float32).astype(
        jnp.bfloat16
    )
    picked = picked.reshape(leading + (2,) + table.shape[1:])
    picked = jnp.moveaxis(picked, -3, -2)
    return picked.reshape(leading + table.shape[1:-1] + (2 * table.shape[-1],))


def smooth_deep(current, row_index, col_index, row_count, col_count):
    rows_here = current.shape[1]
    cols_here = current.shape[2]
    extended = with_halo(current, (("row", 1), ("col", 2)), TV_STEPS)
    for repeat in range(TV_STEPS):
        margin = TV_STEPS - repeat - 1
        inner = extended[:, 1:-1, 1:-1] - descent_step * tv_gradient(extended)
        row_place = (
            row_index * rows_here - margin + jnp.arange(rows_here + 2 * margin, dtype=jnp.int32)
        )
        col_place = (
            col_index * cols_here - margin + jnp.arange(cols_here + 2 * margin, dtype=jnp.int32)
        )
        row_inside = (row_place >= 0) & (row_place < rows_here * row_count)
        col_inside = (col_place >= 0) & (col_place < cols_here * col_count)
        inside = row_inside[:, None] & col_inside[None, :]
        extended = jnp.where(inside[None], inner, jnp.float32(0.0))
    return extended


def local(current_image, measured, ray_weight, angle_ids, shadow_start):
    row_index = lax.axis_index("row")
    col_index = lax.axis_index("col")
    row_count = lax.axis_size("row")
    col_count = lax.axis_size("col")
    slices = current_image.shape[0]
    local_width = current_image.shape[2]
    across = local_width // TILE
    angles_here = ANGLES // col_count
    table = angle_table(angle_ids)
    rows = current_image.transpose(1, 0, 2)
    columns = current_image.reshape(slices, TILE, across, TILE).transpose(3, 0, 2, 1)
    lines = jnp.stack([rows, columns.reshape(TILE, slices, local_width)])
    row_starts = shadow_start[row_index]
    own_starts = lax.dynamic_slice_in_dim(row_starts, col_index * across, across, 0)

    partial_value = project(lines, table)
    entries = place(
        partial_value.reshape(ANGLES * across, slices, TILE), (own_starts.T % TILE).reshape(-1)
    )
    entries = entries.reshape(ANGLES, across, slices, 2, TILE).transpose(0, 1, 3, 2, 4)
    pair_index = jnp.arange(2, dtype=jnp.int32)
    blocks = (own_starts.T // TILE)[:, :, None] + pair_index[None, None, :]
    target = blocks * ANGLES + jnp.arange(ANGLES, dtype=jnp.int32)[:, None, None]
    targets_all = jnp.arange(row_count * ANGLES, dtype=jnp.int32)
    onehot = (targets_all[:, None] == target.reshape(1, -1)).astype(jnp.float32)
    dense_sums = jnp.dot(
        onehot,
        entries.reshape(ANGLES * across * 2, slices * TILE),
        precision=lax.Precision.HIGHEST,
        preferred_element_type=jnp.float32,
    )
    ray_sums = lax.psum_scatter(dense_sums, ("row", "col"), scatter_dimension=0, tiled=True)
    ray_sums = ray_sums.reshape(angles_here, 1, slices, TILE)
    residual = ray_weight[:, :, None, :] * (measured - ray_sums)
    padded = with_halo(residual, (("row", 1),), 1)
    in_bins = jnp.arange(TILE, dtype=jnp.int32)
    filtered = jnp.zeros((angles_here * slices, TILE), jnp.float32)
    for neighbour in (-1, 0, 1):
        ramp_block = ramp(in_bins[None, :] - in_bins[:, None] - neighbour * TILE)
        filtered = filtered + jnp.dot(
            padded[:, 1 + neighbour].reshape(-1, TILE),
            ramp_block,
            precision=lax.Precision.HIGHEST,
            preferred_element_type=jnp.float32,
        )
    filtered = filtered.astype(jnp.bfloat16).reshape(angles_here, slices, TILE)
    sinogram = lax.all_gather(filtered, ("row", "col"), axis=0, tiled=True)
    blocks = own_starts.T // TILE
    angle_rows = jnp.arange(ANGLES, dtype=jnp.int32)[:, None]
    first_rows = blocks * ANGLES + angle_rows
    second = jnp.minimum(blocks + 1, row_count - 1) * ANGLES + angle_rows
    two_blocks = pick_rows(sinogram, first_rows, second)
    shadows = window(two_blocks, own_starts.T % TILE)

    current = back_project(shadows, rows, table).transpose(1, 0, 2)
    current = smooth_deep(current, row_index, col_index, row_count, col_count)
    return current


def solution(mesh):
    return jax.shard_map(
        local,
        mesh=mesh,
        in_specs=(
            P(None, "row", "col"),
            P("col", "row", None, None),
            P("col", "row", None),
            P(),
            P(),
        ),
        out_specs=P(None, "row", "col"),
        check_vma=False,
    )
```

```python
import math

import jax
import jax.numpy as jnp
from jax import lax
from jax.experimental import pallas as pl
from jax.experimental.pallas import tpu as pltpu
from jax.sharding import PartitionSpec as P

TILE = 128
ANGLES = 16
ALL_ANGLES = 256
TV_STEPS = 4


inverse_root = 0.7071067811865476
proj_scale = 0.03125
relaxation = 8.0
smoothing = 0.25
descent_step = 0.05


def with_halo(value, sides, width):
    for axis, dim in sides:
        peers, length = (lax.axis_size(axis), value.shape[dim])
        up = [(i, (i + 1) % peers) for i in range(peers - 1)]
        down = [(j, i) for i, j in up]
        last = lax.slice_in_dim(value, length - width, length, axis=dim)
        initial = lax.slice_in_dim(value, 0, width, axis=dim)
        before = lax.ppermute(last, axis, up)
        after = lax.ppermute(initial, axis, down)
        value = jnp.concatenate([before, value, after], axis=dim)
    return value


def angle_table(angle_ids):
    radians = angle_ids.astype(jnp.float32) * (math.pi / ALL_ANGLES)
    row_step = jnp.cos(radians) * inverse_root
    col_step = jnp.sin(radians) * inverse_root
    steep = jnp.where(jnp.abs(col_step) >= jnp.abs(row_step), 0, 1).astype(jnp.int32)
    return row_step, col_step, steep


def lookup(table, index):
    return jnp.take_along_axis(table, index, axis=1, mode="promise_in_bounds")


def pieces(slices, across):
    return [(t, g) for t in range(across) for g in range(slices // 8)]


LINES = 8


def forward_kernel(slow_ref, fast_ref, steep_ref, shift_ref, x_ref, out_ref):
    slices = x_ref.shape[2]
    across = x_ref.shape[3] // TILE
    parts = pieces(slices, across)
    centre = (TILE - 1) / 2.0
    whole_lanes = lax.broadcasted_iota(jnp.int32, (8, TILE), 1)
    lanes = whole_lanes.astype(jnp.float32)

    def one_angle(a, carry):
        slow = slow_ref[a]
        fast = fast_ref[a]
        steep = steep_ref[a]
        inverse = 1.0 / jnp.full((8, TILE), fast, jnp.float32)
        b = jnp.abs(jnp.full((8, TILE), fast, jnp.float32))
        one_b = 1.0 - b
        two_b = 1.0 - 2.0 * b
        base = (lanes + (0.5 - TILE / 2.0)) * inverse + centre
        tilt = slow * inverse

        def some_lines(block, sums):
            sums = list(sums)
            for k in range(LINES):
                line = block * LINES + k
                q = base - (line.astype(jnp.float32) - centre) * tilt
                whole = jnp.floor(q)
                t = b * (q - whole)
                first = whole.astype(jnp.int32) - 1
                weights = (
                    jnp.maximum(one_b - t, 0.0),
                    1.0 - t,
                    one_b + t,
                    jnp.maximum(two_b + t, 0.0),
                )
                picks = []
                for j, w in enumerate(weights):
                    at = first + j
                    index = at & (TILE - 1)
                    picks.append((index, jnp.where(index == at, w, 0.0)))
                for n, (tile, group) in enumerate(parts):
                    row = x_ref[
                        steep, line, group * 8 : group * 8 + 8, tile * TILE : (tile + 1) * TILE
                    ]
                    (i0, w0), (i1, w1), (i2, w2), (i3, w3) = picks
                    sums[n] = sums[n] + (
                        (lookup(row, i0) * w0 + lookup(row, i1) * w1)
                        + (lookup(row, i2) * w2 + lookup(row, i3) * w3)
                    )
            return tuple(sums)

        zero = jnp.zeros((8, TILE), jnp.float32)
        sums = lax.fori_loop(0, TILE // LINES, some_lines, (zero,) * len(parts))
        for n, (tile, group) in enumerate(parts):
            turned = lookup(sums[n], (whole_lanes - shift_ref[a, tile]) & (TILE - 1))
            out_ref[a, tile, group * 8 : group * 8 + 8, :] = turned * proj_scale
        return carry

    lax.fori_loop(0, slow_ref.shape[0], one_angle, jnp.int32(0))


def project(lines, table, shift):
    row_step, col_step, steep = table
    slow = jnp.where(steep == 0, row_step, col_step)
    fast = jnp.where(steep == 0, col_step, row_step)
    slices = lines.shape[2]
    across = lines.shape[3] // TILE
    smem = pl.BlockSpec(memory_space=pltpu.SMEM)
    vmem = pl.BlockSpec(memory_space=pltpu.VMEM)
    return pl.pallas_call(
        forward_kernel,
        out_shape=jax.ShapeDtypeStruct((ANGLES, across, slices, TILE), jnp.float32),
        in_specs=[smem, smem, smem, smem, vmem],
        out_specs=vmem,
        name="project",
    )(slow, fast, steep, shift, lines)


def backward_kernel(row_ref, col_ref, shift_ref, shadow_ref, x_ref, out_ref, value_ref, step_ref, base_ref):
    slices = x_ref.shape[1]
    across = x_ref.shape[2] // TILE
    angles = shadow_ref.shape[0]
    parts = pieces(slices, across)
    centre = (TILE - 1) / 2.0
    whole_lanes = lax.broadcasted_iota(jnp.int32, (8, TILE), 1)
    lanes = whole_lanes.astype(jnp.float32) - centre
    scale = relaxation * proj_scale
    for a in range(angles):
        base_ref[a] = TILE / 2.0 - 0.5 + lanes * col_ref[a]
        for n, (tile, group) in enumerate(parts):
            value = shadow_ref[a, tile, group * 8 : group * 8 + 8, :].astype(jnp.float32) * scale
            value = lookup(value, (whole_lanes + shift_ref[a, tile]) & (TILE - 1))
            value_ref[a, n] = value
            step_ref[a, n] = jnp.roll(value, -1, axis=1) - value

    def one_row(u, carry):
        place = u.astype(jnp.float32) - centre
        sums = [
            x_ref[u, g * 8 : g * 8 + 8, t * TILE : (t + 1) * TILE].astype(jnp.float32)
            for t, g in parts
        ]
        for a in range(angles):
            z = base_ref[a] + place * row_ref[a]
            z = jnp.minimum(jnp.maximum(z, 0.0), TILE - 1.00001)
            whole = jnp.floor(z)
            part = z - whole
            index = whole.astype(jnp.int32)
            for n in range(len(parts)):
                sums[n] = sums[n] + (
                    lookup(value_ref[a, n], index) + part * lookup(step_ref[a, n], index)
                )
        for n, (t, g) in enumerate(parts):
            out_ref[u, g * 8 : g * 8 + 8, t * TILE : (t + 1) * TILE] = sums[n]
        return carry

    lax.fori_loop(0, TILE, one_row, jnp.int32(0))


def back_project(shadows, rows, table, shift):
    row_step, col_step, steep = table
    angles, across, slices, unused = shadows.shape
    smem = pl.BlockSpec(memory_space=pltpu.SMEM)
    vmem = pl.BlockSpec(memory_space=pltpu.VMEM)
    parts = across * slices // 8
    return pl.pallas_call(
        backward_kernel,
        out_shape=jax.ShapeDtypeStruct(rows.shape, jnp.float32),
        in_specs=[smem, smem, smem, vmem, vmem],
        out_specs=vmem,
        scratch_shapes=[
            pltpu.VMEM((angles, parts, 8, TILE), jnp.float32),
            pltpu.VMEM((angles, parts, 8, TILE), jnp.float32),
            pltpu.VMEM((angles, 8, TILE), jnp.float32),
        ],
        name="back_project",
    )(row_step, col_step, shift, shadows, rows)


def ramp(offset):
    is_odd = offset % 2 != 0
    nonzero = jnp.where(offset == 0, 1, offset).astype(jnp.float32)
    values = jnp.where(is_odd, -1.0 / (math.pi * math.pi * nonzero * nonzero), 0.0)
    values = jnp.where(offset == 0, 0.25, values)
    return jnp.where(jnp.abs(offset) < TILE, values, 0.0)


MESH = pl.DeviceIdType.MESH


def exchange_kernel(
    partial_ref,
    target_ref,
    measured_ref,
    weight_ref,
    ramp_ref,
    out_ref,
    tiles,
    outgoing,
    incoming,
    residual,
    filtered,
    windows,
    landed,
    tile_sems,
    sum_sems,
    edge_sems,
    filter_sems,
    window_sems,
):
    row_count = lax.axis_size("row")
    col_count = lax.axis_size("col")
    row = lax.axis_index("row")
    col = lax.axis_index("col")
    here = measured_ref.shape[0]

    def send(src, dst, sems, k, to_row, to_col):
        return pltpu.make_async_remote_copy(
            src_ref=src,
            dst_ref=dst,
            send_sem=sems.at[0, k],
            recv_sem=sems.at[1, k],
            device_id=(to_row, to_col),
            device_id_type=MESH,
        )

    barrier = pltpu.get_barrier_semaphore()
    for k in range(1, col_count):
        pl.semaphore_signal(
            barrier, inc=1, device_id=(row, lax.rem(col + k, col_count)), device_id_type=MESH
        )
    for k in range(1, row_count):
        pl.semaphore_signal(
            barrier, inc=1, device_id=(lax.rem(row + k, row_count), col), device_id_type=MESH
        )
    pl.semaphore_wait(barrier, col_count + row_count - 2)

    copies = []
    for k in range(1, col_count):
        peer = lax.rem(col + k, col_count)
        copies.append(
            send(partial_ref.at[peer], tiles.at[col], tile_sems, k, row, peer)
        )
        copies[-1].start()
    tiles[col] = partial_ref[col]
    for k in range(1, col_count):
        copies[k - 1].wait_recv()

    def summed(block):
        chosen = jnp.where(target_ref[...] == block, tiles[...], 0.0)
        return jnp.sum(jnp.sum(chosen, axis=2), axis=0)

    sums = []
    for k in range(1, row_count):
        peer = lax.rem(row + k, row_count)
        outgoing[k] = summed(peer)
        sums.append(send(outgoing.at[k], incoming.at[k], sum_sems, k, peer, col))
        sums[-1].start()
    total = summed(row)
    for k in range(1, row_count):
        sums[k - 1].wait_recv()
        total = total + incoming[k]
    residual[1] = weight_ref[...] * (measured_ref[...] - total)

    before = send(residual.at[1], residual.at[2], edge_sems, 0, row - 1, col)
    after = send(residual.at[1], residual.at[0], edge_sems, 1, row + 1, col)

    @pl.when(row > 0)
    def _():
        before.start()

    @pl.when(row < row_count - 1)
    def _():
        after.start()

    @pl.when(row == 0)
    def _():
        residual[0] = jnp.zeros(residual.shape[1:], jnp.float32)

    @pl.when(row == row_count - 1)
    def _():
        residual[2] = jnp.zeros(residual.shape[1:], jnp.float32)

    def ramped(n):
        flat = residual[n].reshape(-1, TILE)
        return jnp.dot(
            flat,
            ramp_ref[n],
            precision=lax.Precision.HIGHEST,
            preferred_element_type=jnp.float32,
        )

    result = ramped(1)

    @pl.when(row > 0)
    def _():
        after.wait_recv()

    @pl.when(row < row_count - 1)
    def _():
        before.wait_recv()

    result = result + ramped(0) + ramped(2)
    filtered[row] = result.astype(jnp.bfloat16).reshape(filtered.shape[1:])

    gathers = []
    for k in range(1, row_count):
        peer = lax.rem(row + k, row_count)
        gathers.append(send(filtered.at[row], filtered.at[row], filter_sems, k, peer, col))
        gathers[-1].start()
    for k in range(1, row_count):
        source = lax.rem(row + row_count - k, row_count)
        send(
            filtered.at[source], filtered.at[source], filter_sems, k, source, col
        ).wait_recv()

    def window(peer):
        target = target_ref[peer]
        value = jnp.zeros(target.shape, jnp.float32)
        for block in range(row_count):
            piece = filtered[block].astype(jnp.float32)[:, None]
            value = jnp.where(target == block, piece, value)
        return value.astype(jnp.bfloat16)

    moves = []
    for k in range(1, col_count):
        peer = lax.rem(col + k, col_count)
        windows[k] = window(peer)
        moves.append(send(windows.at[k], landed.at[col], window_sems, k, row, peer))
        moves[-1].start()
    landed[col] = window(col)
    for move in moves:
        move.wait_recv()
    out_ref[...] = landed[...]

    for copy in copies + sums + gathers + moves:
        copy.wait_send()

    @pl.when(row > 0)
    def _():
        before.wait_send()

    @pl.when(row < row_count - 1)
    def _():
        after.wait_send()


def exchange(partial_value, target, measured, ray_weight):
    row_count = lax.axis_size("row")
    col_count = lax.axis_size("col")
    angles, across, slices, unused = partial_value.shape
    here = angles // col_count
    in_bins = jnp.arange(TILE, dtype=jnp.int32)
    ramps = jnp.stack(
        [ramp(in_bins[None, :] - in_bins[:, None] - n * TILE) for n in (-1, 0, 1)]
    )
    shape = (col_count, here, across, slices, TILE)
    dma = pltpu.SemaphoreType.DMA
    vmem = pl.BlockSpec(memory_space=pltpu.VMEM)
    target = jnp.broadcast_to(target[:, :, :, None, :], shape)
    block = (here, slices, TILE)
    result = pl.pallas_call(
        exchange_kernel,
        out_shape=jax.ShapeDtypeStruct(shape, jnp.bfloat16),
        in_specs=[vmem] * 5,
        out_specs=vmem,
        scratch_shapes=[
            pltpu.VMEM(shape, jnp.float32),
            pltpu.VMEM((row_count,) + block, jnp.float32),
            pltpu.VMEM((row_count,) + block, jnp.float32),
            pltpu.VMEM((3,) + block, jnp.float32),
            pltpu.VMEM((row_count,) + block, jnp.bfloat16),
            pltpu.VMEM(shape, jnp.bfloat16),
            pltpu.VMEM(shape, jnp.bfloat16),
            dma((2, col_count)),
            dma((2, row_count)),
            dma((2, 2)),
            dma((2, row_count)),
            dma((2, col_count)),
        ],
        compiler_params=pltpu.CompilerParams(collective_id=0, has_side_effects=True),
        name="exchange",
    )(
        partial_value.reshape(shape),
        target,
        measured.reshape(block),
        ray_weight.reshape(here, 1, TILE),
        ramps,
    )
    return result.reshape(partial_value.shape)


def tv_gradient(padded):
    corner = padded[:, :-1, :-1]
    step_down = padded[:, 1:, :-1] - corner
    step_right = padded[:, :-1, 1:] - corner
    magnitude = jnp.sqrt(smoothing * smoothing + step_down * step_down + step_right * step_right)
    flow_down = step_down / magnitude
    flow_right = step_right / magnitude
    return (
        flow_down[:, :-1, 1:]
        - flow_down[:, 1:, 1:]
        + flow_right[:, 1:, :-1]
        - flow_right[:, 1:, 1:]
    )


def smooth_deep(current, row_index, col_index, row_count, col_count):
    rows_here = current.shape[1]
    cols_here = current.shape[2]
    extended = with_halo(current, (("row", 1), ("col", 2)), TV_STEPS)
    for repeat in range(TV_STEPS):
        margin = TV_STEPS - repeat - 1
        inner = extended[:, 1:-1, 1:-1] - descent_step * tv_gradient(extended)
        row_place = (
            row_index * rows_here - margin + jnp.arange(rows_here + 2 * margin, dtype=jnp.int32)
        )
        col_place = (
            col_index * cols_here - margin + jnp.arange(cols_here + 2 * margin, dtype=jnp.int32)
        )
        row_inside = (row_place >= 0) & (row_place < rows_here * row_count)
        col_inside = (col_place >= 0) & (col_place < cols_here * col_count)
        inside = row_inside[:, None] & col_inside[None, :]
        extended = jnp.where(inside[None], inner, jnp.float32(0.0))
    return extended


def local(current_image, measured, ray_weight, angle_ids, shadow_start):
    row_index = lax.axis_index("row")
    col_index = lax.axis_index("col")
    row_count = lax.axis_size("row")
    col_count = lax.axis_size("col")
    slices = current_image.shape[0]
    local_width = current_image.shape[2]
    across = local_width // TILE
    angles_here = ANGLES // col_count
    table = angle_table(angle_ids)
    rows = current_image.transpose(1, 0, 2)
    columns = current_image.reshape(slices, TILE, across, TILE).transpose(3, 0, 2, 1)
    lines = jnp.stack([rows, columns.reshape(TILE, slices, local_width)])
    row_starts = shadow_start[row_index]
    own_starts = lax.dynamic_slice_in_dim(row_starts, col_index * across, across, 0)

    shift = own_starts.T % TILE
    partial_value = project(lines, table, shift)
    wanted = lax.dynamic_slice_in_dim(row_starts, col_index * angles_here, angles_here, 1)
    lane = jnp.arange(TILE, dtype=jnp.int32)
    target = wanted[:, :, None] // TILE + (lane < wanted[:, :, None] % TILE)
    target = target.reshape(col_count, across, angles_here, TILE).transpose(0, 2, 1, 3)
    shadows = exchange(partial_value, target.astype(jnp.int32), measured, ray_weight)
    current = back_project(shadows, rows, table, shift).transpose(1, 0, 2)
    current = smooth_deep(current, row_index, col_index, row_count, col_count)
    return current


def solution(mesh):
    return jax.shard_map(
        local,
        mesh=mesh,
        in_specs=(
            P(None, "row", "col"),
            P("col", "row", None, None),
            P("col", "row", None),
            P(),
            P(),
        ),
        out_specs=P(None, "row", "col"),
        check_vma=False,
    )
```

```python
import math

import jax
import jax.numpy as jnp
from jax import lax
from jax.experimental import pallas as pl
from jax.experimental.pallas import tpu as pltpu
from jax.sharding import PartitionSpec as P

TILE = 128
ANGLES = 16
ALL_ANGLES = 256
TV_STEPS = 4


inverse_root = 0.7071067811865476
proj_scale = 0.03125
relaxation = 8.0
smoothing = 0.25
descent_step = 0.05


def with_halo(value, sides, width):
    for axis, dim in sides:
        peers, length = (lax.axis_size(axis), value.shape[dim])
        up = [(i, (i + 1) % peers) for i in range(peers - 1)]
        down = [(j, i) for i, j in up]
        last = lax.slice_in_dim(value, length - width, length, axis=dim)
        initial = lax.slice_in_dim(value, 0, width, axis=dim)
        before = lax.ppermute(last, axis, up)
        after = lax.ppermute(initial, axis, down)
        value = jnp.concatenate([before, value, after], axis=dim)
    return value


def angle_table(angle_ids):
    radians = angle_ids.astype(jnp.float32) * (math.pi / ALL_ANGLES)
    row_step = jnp.cos(radians) * inverse_root
    col_step = jnp.sin(radians) * inverse_root
    steep = jnp.where(jnp.abs(col_step) >= jnp.abs(row_step), 0, 1).astype(jnp.int32)
    return row_step, col_step, steep


def lookup(table, index):
    return jnp.take_along_axis(table, index, axis=1, mode="promise_in_bounds")


def pieces(slices, across):
    return [(t, g) for t in range(across) for g in range(slices // 8)]


LINES = 8


def forward_kernel(
    slow_ref, fast_ref, steep_ref, shift_ref, x_ref, prefix_ref, out_ref, once_ref, twice_ref
):
    slices = x_ref.shape[2]
    across = x_ref.shape[3] // TILE
    groups = slices // 8
    count = across * groups
    centre = (TILE - 1) / 2.0
    whole_lanes = lax.broadcasted_iota(jnp.int32, (8, TILE), 1)
    lanes = whole_lanes.astype(jnp.float32)
    following = (whole_lanes + 1) & (TILE - 1)
    preceding = (whole_lanes - 1) & (TILE - 1)

    def fill(block, carry):
        at = pl.multiple_of(block * LINES, LINES)
        for way in range(2):
            for tile in range(across):
                flat = x_ref[way, pl.ds(at, LINES), :, tile * TILE : (tile + 1) * TILE]
                both = jnp.dot(
                    flat.reshape(LINES * slices, TILE),
                    prefix_ref[...],
                    preferred_element_type=jnp.float32,
                ).reshape(LINES, groups, 8, 2 * TILE)
                span = slice(tile * groups, (tile + 1) * groups)
                once_ref[way, pl.ds(at, LINES), span] = both[..., :TILE]
                twice_ref[way, pl.ds(at, LINES), span] = both[..., TILE:]
        return carry

    lax.fori_loop(0, TILE // LINES, fill, jnp.int32(0))
    zero = jnp.zeros((8, TILE), jnp.float32)

    def add_line(line, sums):
        return tuple(sums[n] + once_ref[0, line, n] for n in range(count))

    totals = lax.fori_loop(0, TILE, add_line, (zero,) * count)
    totals = [lookup(t, jnp.full((8, TILE), TILE - 1, jnp.int32)) for t in totals]

    def one_angle(a, carry):
        slow = slow_ref[a]
        fast = jnp.full((8, TILE), fast_ref[a], jnp.float32)
        steep = steep_ref[a]
        inverse = 1.0 / fast
        base = (lanes + (0.5 - TILE / 2.0)) * inverse + centre
        tilt = slow * inverse

        def some_lines(block, sums):
            here = [zero] * count
            for k in range(LINES):
                line = block * LINES + k
                q = jnp.maximum(base - (line.astype(jnp.float32) - centre) * tilt, 0.0)
                whole = jnp.minimum(jnp.floor(q), TILE - 1.0)
                part = q - whole
                index = whole.astype(jnp.int32)
                first = [lookup(once_ref[steep, line, n], index) for n in range(count)]
                second = [lookup(twice_ref[steep, line, n], index) for n in range(count)]
                for n in range(count):
                    here[n] = here[n] + (second[n] + part * first[n])
            return tuple(
                sums[n] + (lookup(here[n], following) - here[n]) for n in range(count)
            )

        sums = lax.fori_loop(0, TILE // LINES, some_lines, (zero,) * count)
        for n in range(count):
            tile, group = n // groups, n % groups
            beyond = totals[n] * inverse
            last = jnp.where(fast > 0, beyond, 0.0)
            before = jnp.where(fast > 0, 0.0, beyond)
            steps = jnp.where(whole_lanes == TILE - 1, last, sums[n])
            earlier = jnp.where(whole_lanes == 0, before, lookup(steps, preceding))
            shadow = (steps - earlier) * (jnp.abs(fast) * proj_scale)
            turned = lookup(shadow, (whole_lanes - shift_ref[a, tile]) & (TILE - 1))
            out_ref[a, tile, group * 8 : group * 8 + 8, :] = turned
        return carry

    lax.fori_loop(0, slow_ref.shape[0], one_angle, jnp.int32(0))


def project(lines, table, shift):
    row_step, col_step, steep = table
    slow = jnp.where(steep == 0, row_step, col_step)
    fast = jnp.where(steep == 0, col_step, row_step)
    slices = lines.shape[2]
    across = lines.shape[3] // TILE
    spot = jnp.arange(TILE, dtype=jnp.int32)
    gap = spot[None, :] - spot[:, None]
    prefix = jnp.concatenate([gap >= 0, jnp.maximum(gap, 0)], axis=1).astype(jnp.bfloat16)
    smem = pl.BlockSpec(memory_space=pltpu.SMEM)
    vmem = pl.BlockSpec(memory_space=pltpu.VMEM)
    held = pltpu.VMEM((2, TILE, across * slices // 8, 8, TILE), jnp.float32)
    return pl.pallas_call(
        forward_kernel,
        out_shape=jax.ShapeDtypeStruct((ANGLES, across, slices, TILE), jnp.float32),
        in_specs=[smem, smem, smem, smem, vmem, vmem],
        out_specs=vmem,
        scratch_shapes=[held, held],
        compiler_params=pltpu.CompilerParams(vmem_limit_bytes=48 << 20),
        name="project",
    )(slow, fast, steep, shift, lines, prefix)


def backward_kernel(row_ref, col_ref, shift_ref, shadow_ref, x_ref, out_ref, value_ref, step_ref, base_ref):
    slices = x_ref.shape[1]
    across = x_ref.shape[2] // TILE
    angles = shadow_ref.shape[0]
    parts = pieces(slices, across)
    centre = (TILE - 1) / 2.0
    whole_lanes = lax.broadcasted_iota(jnp.int32, (8, TILE), 1)
    lanes = whole_lanes.astype(jnp.float32) - centre
    scale = relaxation * proj_scale
    for a in range(angles):
        base_ref[a] = TILE / 2.0 - 0.5 + lanes * col_ref[a]
        for n, (tile, group) in enumerate(parts):
            value = shadow_ref[a, tile, group * 8 : group * 8 + 8, :].astype(jnp.float32) * scale
            value = lookup(value, (whole_lanes + shift_ref[a, tile]) & (TILE - 1))
            value_ref[a, n] = value
            step_ref[a, n] = jnp.roll(value, -1, axis=1) - value

    def one_row(u, carry):
        place = u.astype(jnp.float32) - centre
        sums = [
            x_ref[u, g * 8 : g * 8 + 8, t * TILE : (t + 1) * TILE].astype(jnp.float32)
            for t, g in parts
        ]
        for a in range(angles):
            z = base_ref[a] + place * row_ref[a]
            z = jnp.minimum(jnp.maximum(z, 0.0), TILE - 1.00001)
            whole = jnp.floor(z)
            part = z - whole
            index = whole.astype(jnp.int32)
            for n in range(len(parts)):
                sums[n] = sums[n] + (
                    lookup(value_ref[a, n], index) + part * lookup(step_ref[a, n], index)
                )
        for n, (t, g) in enumerate(parts):
            out_ref[u, g * 8 : g * 8 + 8, t * TILE : (t + 1) * TILE] = sums[n]
        return carry

    lax.fori_loop(0, TILE, one_row, jnp.int32(0))


def back_project(shadows, rows, table, shift):
    row_step, col_step, steep = table
    angles, across, slices, unused = shadows.shape
    smem = pl.BlockSpec(memory_space=pltpu.SMEM)
    vmem = pl.BlockSpec(memory_space=pltpu.VMEM)
    parts = across * slices // 8
    return pl.pallas_call(
        backward_kernel,
        out_shape=jax.ShapeDtypeStruct(rows.shape, jnp.float32),
        in_specs=[smem, smem, smem, vmem, vmem],
        out_specs=vmem,
        scratch_shapes=[
            pltpu.VMEM((angles, parts, 8, TILE), jnp.float32),
            pltpu.VMEM((angles, parts, 8, TILE), jnp.float32),
            pltpu.VMEM((angles, 8, TILE), jnp.float32),
        ],
        name="back_project",
    )(row_step, col_step, shift, shadows, rows)


def ramp(offset):
    is_odd = offset % 2 != 0
    nonzero = jnp.where(offset == 0, 1, offset).astype(jnp.float32)
    values = jnp.where(is_odd, -1.0 / (math.pi * math.pi * nonzero * nonzero), 0.0)
    values = jnp.where(offset == 0, 0.25, values)
    return jnp.where(jnp.abs(offset) < TILE, values, 0.0)


MESH = pl.DeviceIdType.MESH


def exchange_kernel(
    partial_ref,
    target_ref,
    measured_ref,
    weight_ref,
    ramp_ref,
    out_ref,
    tiles,
    outgoing,
    incoming,
    residual,
    filtered,
    windows,
    landed,
    tile_sems,
    sum_sems,
    edge_sems,
    filter_sems,
    window_sems,
):
    row_count = lax.axis_size("row")
    col_count = lax.axis_size("col")
    row = lax.axis_index("row")
    col = lax.axis_index("col")
    here = measured_ref.shape[0]

    def send(src, dst, sems, k, to_row, to_col):
        return pltpu.make_async_remote_copy(
            src_ref=src,
            dst_ref=dst,
            send_sem=sems.at[0, k],
            recv_sem=sems.at[1, k],
            device_id=(to_row, to_col),
            device_id_type=MESH,
        )

    barrier = pltpu.get_barrier_semaphore()
    for k in range(1, col_count):
        pl.semaphore_signal(
            barrier, inc=1, device_id=(row, lax.rem(col + k, col_count)), device_id_type=MESH
        )
    for k in range(1, row_count):
        pl.semaphore_signal(
            barrier, inc=1, device_id=(lax.rem(row + k, row_count), col), device_id_type=MESH
        )
    pl.semaphore_wait(barrier, col_count + row_count - 2)

    copies = []
    for k in range(1, col_count):
        peer = lax.rem(col + k, col_count)
        copies.append(
            send(partial_ref.at[peer], tiles.at[col], tile_sems, k, row, peer)
        )
        copies[-1].start()
    tiles[col] = partial_ref[col]
    for k in range(1, col_count):
        copies[k - 1].wait_recv()

    def summed(block):
        chosen = jnp.where(target_ref[...] == block, tiles[...], 0.0)
        return jnp.sum(jnp.sum(chosen, axis=2), axis=0)

    sums = []
    for k in range(1, row_count):
        peer = lax.rem(row + k, row_count)
        outgoing[k] = summed(peer)
        sums.append(send(outgoing.at[k], incoming.at[k], sum_sems, k, peer, col))
        sums[-1].start()
    total = summed(row)
    for k in range(1, row_count):
        sums[k - 1].wait_recv()
        total = total + incoming[k]
    residual[1] = weight_ref[...] * (measured_ref[...] - total)

    before = send(residual.at[1], residual.at[2], edge_sems, 0, row - 1, col)
    after = send(residual.at[1], residual.at[0], edge_sems, 1, row + 1, col)

    @pl.when(row > 0)
    def _():
        before.start()

    @pl.when(row < row_count - 1)
    def _():
        after.start()

    @pl.when(row == 0)
    def _():
        residual[0] = jnp.zeros(residual.shape[1:], jnp.float32)

    @pl.when(row == row_count - 1)
    def _():
        residual[2] = jnp.zeros(residual.shape[1:], jnp.float32)

    def ramped(n):
        flat = residual[n].reshape(-1, TILE)
        return jnp.dot(
            flat,
            ramp_ref[n],
            precision=lax.Precision.HIGHEST,
            preferred_element_type=jnp.float32,
        )

    result = ramped(1)

    @pl.when(row > 0)
    def _():
        after.wait_recv()

    @pl.when(row < row_count - 1)
    def _():
        before.wait_recv()

    result = result + ramped(0) + ramped(2)
    filtered[row] = result.astype(jnp.bfloat16).reshape(filtered.shape[1:])

    gathers = []
    for k in range(1, row_count):
        peer = lax.rem(row + k, row_count)
        gathers.append(send(filtered.at[row], filtered.at[row], filter_sems, k, peer, col))
        gathers[-1].start()
    for k in range(1, row_count):
        source = lax.rem(row + row_count - k, row_count)
        send(
            filtered.at[source], filtered.at[source], filter_sems, k, source, col
        ).wait_recv()

    def window(peer):
        target = target_ref[peer]
        value = jnp.zeros(target.shape, jnp.float32)
        for block in range(row_count):
            piece = filtered[block].astype(jnp.float32)[:, None]
            value = jnp.where(target == block, piece, value)
        return value.astype(jnp.bfloat16)

    moves = []
    for k in range(1, col_count):
        peer = lax.rem(col + k, col_count)
        windows[k] = window(peer)
        moves.append(send(windows.at[k], landed.at[col], window_sems, k, row, peer))
        moves[-1].start()
    landed[col] = window(col)
    for move in moves:
        move.wait_recv()
    out_ref[...] = landed[...]

    for copy in copies + sums + gathers + moves:
        copy.wait_send()

    @pl.when(row > 0)
    def _():
        before.wait_send()

    @pl.when(row < row_count - 1)
    def _():
        after.wait_send()


def exchange(partial_value, target, measured, ray_weight):
    row_count = lax.axis_size("row")
    col_count = lax.axis_size("col")
    angles, across, slices, unused = partial_value.shape
    here = angles // col_count
    in_bins = jnp.arange(TILE, dtype=jnp.int32)
    ramps = jnp.stack(
        [ramp(in_bins[None, :] - in_bins[:, None] - n * TILE) for n in (-1, 0, 1)]
    )
    shape = (col_count, here, across, slices, TILE)
    dma = pltpu.SemaphoreType.DMA
    vmem = pl.BlockSpec(memory_space=pltpu.VMEM)
    target = jnp.broadcast_to(target[:, :, :, None, :], shape)
    block = (here, slices, TILE)
    result = pl.pallas_call(
        exchange_kernel,
        out_shape=jax.ShapeDtypeStruct(shape, jnp.bfloat16),
        in_specs=[vmem] * 5,
        out_specs=vmem,
        scratch_shapes=[
            pltpu.VMEM(shape, jnp.float32),
            pltpu.VMEM((row_count,) + block, jnp.float32),
            pltpu.VMEM((row_count,) + block, jnp.float32),
            pltpu.VMEM((3,) + block, jnp.float32),
            pltpu.VMEM((row_count,) + block, jnp.bfloat16),
            pltpu.VMEM(shape, jnp.bfloat16),
            pltpu.VMEM(shape, jnp.bfloat16),
            dma((2, col_count)),
            dma((2, row_count)),
            dma((2, 2)),
            dma((2, row_count)),
            dma((2, col_count)),
        ],
        compiler_params=pltpu.CompilerParams(collective_id=0, has_side_effects=True),
        name="exchange",
    )(
        partial_value.reshape(shape),
        target,
        measured.reshape(block),
        ray_weight.reshape(here, 1, TILE),
        ramps,
    )
    return result.reshape(partial_value.shape)


def tv_gradient(padded):
    corner = padded[:, :-1, :-1]
    step_down = padded[:, 1:, :-1] - corner
    step_right = padded[:, :-1, 1:] - corner
    magnitude = jnp.sqrt(smoothing * smoothing + step_down * step_down + step_right * step_right)
    flow_down = step_down / magnitude
    flow_right = step_right / magnitude
    return (
        flow_down[:, :-1, 1:]
        - flow_down[:, 1:, 1:]
        + flow_right[:, 1:, :-1]
        - flow_right[:, 1:, 1:]
    )


def smooth_deep(current, row_index, col_index, row_count, col_count):
    rows_here = current.shape[1]
    cols_here = current.shape[2]
    extended = with_halo(current, (("row", 1), ("col", 2)), TV_STEPS)
    for repeat in range(TV_STEPS):
        margin = TV_STEPS - repeat - 1
        inner = extended[:, 1:-1, 1:-1] - descent_step * tv_gradient(extended)
        row_place = (
            row_index * rows_here - margin + jnp.arange(rows_here + 2 * margin, dtype=jnp.int32)
        )
        col_place = (
            col_index * cols_here - margin + jnp.arange(cols_here + 2 * margin, dtype=jnp.int32)
        )
        row_inside = (row_place >= 0) & (row_place < rows_here * row_count)
        col_inside = (col_place >= 0) & (col_place < cols_here * col_count)
        inside = row_inside[:, None] & col_inside[None, :]
        extended = jnp.where(inside[None], inner, jnp.float32(0.0))
    return extended


def local(current_image, measured, ray_weight, angle_ids, shadow_start):
    row_index = lax.axis_index("row")
    col_index = lax.axis_index("col")
    row_count = lax.axis_size("row")
    col_count = lax.axis_size("col")
    slices = current_image.shape[0]
    local_width = current_image.shape[2]
    across = local_width // TILE
    angles_here = ANGLES // col_count
    table = angle_table(angle_ids)
    rows = current_image.transpose(1, 0, 2)
    rounded = current_image.astype(jnp.bfloat16)
    columns = rounded.reshape(slices, TILE, across, TILE).transpose(3, 0, 2, 1)
    lines = jnp.stack([rounded.transpose(1, 0, 2), columns.reshape(TILE, slices, local_width)])
    row_starts = shadow_start[row_index]
    own_starts = lax.dynamic_slice_in_dim(row_starts, col_index * across, across, 0)

    shift = own_starts.T % TILE
    partial_value = project(lines, table, shift)
    wanted = lax.dynamic_slice_in_dim(row_starts, col_index * angles_here, angles_here, 1)
    lane = jnp.arange(TILE, dtype=jnp.int32)
    target = wanted[:, :, None] // TILE + (lane < wanted[:, :, None] % TILE)
    target = target.reshape(col_count, across, angles_here, TILE).transpose(0, 2, 1, 3)
    shadows = exchange(partial_value, target.astype(jnp.int32), measured, ray_weight)
    current = back_project(shadows, rows, table, shift).transpose(1, 0, 2)
    current = smooth_deep(current, row_index, col_index, row_count, col_count)
    return current


def solution(mesh):
    return jax.shard_map(
        local,
        mesh=mesh,
        in_specs=(
            P(None, "row", "col"),
            P("col", "row", None, None),
            P("col", "row", None),
            P(),
            P(),
        ),
        out_specs=P(None, "row", "col"),
        check_vma=False,
    )
```

```python
import math

import jax
import jax.numpy as jnp
from jax import lax
from jax.experimental import pallas as pl
from jax.experimental.pallas import tpu as pltpu
from jax.sharding import PartitionSpec as P

TILE = 128
ANGLES = 16
ALL_ANGLES = 256
TV_STEPS = 4
PACK = TILE // TV_STEPS


inverse_root = 0.7071067811865476
proj_scale = 0.03125
relaxation = 8.0
smoothing = 0.25
descent_step = 0.05


def angle_table(angle_ids):
    radians = angle_ids.astype(jnp.float32) * (math.pi / ALL_ANGLES)
    row_step = jnp.cos(radians) * inverse_root
    col_step = jnp.sin(radians) * inverse_root
    steep = jnp.where(jnp.abs(col_step) >= jnp.abs(row_step), 0, 1).astype(jnp.int32)
    return row_step, col_step, steep


def lookup(table, index):
    return jnp.take_along_axis(table, index, axis=1, mode="promise_in_bounds")


def pieces(slices, across):
    return [(t, g) for t in range(across) for g in range(slices // 8)]


LINES = 8


def forward_kernel(
    slow_ref, fast_ref, steep_ref, shift_ref, x_ref, prefix_ref, out_ref, once_ref, twice_ref
):
    slices = x_ref.shape[2]
    across = x_ref.shape[3] // TILE
    groups = slices // 8
    count = across * groups
    centre = (TILE - 1) / 2.0
    whole_lanes = lax.broadcasted_iota(jnp.int32, (8, TILE), 1)
    lanes = whole_lanes.astype(jnp.float32)
    following = (whole_lanes + 1) & (TILE - 1)
    preceding = (whole_lanes - 1) & (TILE - 1)

    def fill(block, carry):
        at = pl.multiple_of(block * LINES, LINES)
        for way in range(2):
            for tile in range(across):
                flat = x_ref[way, pl.ds(at, LINES), :, tile * TILE : (tile + 1) * TILE]
                both = jnp.dot(
                    flat.reshape(LINES * slices, TILE),
                    prefix_ref[...],
                    preferred_element_type=jnp.float32,
                ).reshape(LINES, groups, 8, 2 * TILE)
                span = slice(tile * groups, (tile + 1) * groups)
                once_ref[way, pl.ds(at, LINES), span] = both[..., :TILE]
                twice_ref[way, pl.ds(at, LINES), span] = both[..., TILE:]
        return carry

    lax.fori_loop(0, TILE // LINES, fill, jnp.int32(0))
    zero = jnp.zeros((8, TILE), jnp.float32)

    def add_line(line, sums):
        return tuple(sums[n] + once_ref[0, line, n] for n in range(count))

    totals = lax.fori_loop(0, TILE, add_line, (zero,) * count)
    totals = [lookup(t, jnp.full((8, TILE), TILE - 1, jnp.int32)) for t in totals]

    def one_angle(a, carry):
        slow = slow_ref[a]
        fast = jnp.full((8, TILE), fast_ref[a], jnp.float32)
        steep = steep_ref[a]
        inverse = 1.0 / fast
        base = (lanes + (0.5 - TILE / 2.0)) * inverse + centre
        tilt = slow * inverse

        def some_lines(block, sums):
            here = [zero] * count
            for k in range(LINES):
                line = block * LINES + k
                q = jnp.maximum(base - (line.astype(jnp.float32) - centre) * tilt, 0.0)
                whole = jnp.minimum(jnp.floor(q), TILE - 1.0)
                part = q - whole
                index = whole.astype(jnp.int32)
                first = [lookup(once_ref[steep, line, n], index) for n in range(count)]
                second = [lookup(twice_ref[steep, line, n], index) for n in range(count)]
                for n in range(count):
                    here[n] = here[n] + (second[n] + part * first[n])
            return tuple(
                sums[n] + (lookup(here[n], following) - here[n]) for n in range(count)
            )

        sums = lax.fori_loop(0, TILE // LINES, some_lines, (zero,) * count, unroll=4)
        for n in range(count):
            tile, group = n // groups, n % groups
            beyond = totals[n] * inverse
            last = jnp.where(fast > 0, beyond, 0.0)
            before = jnp.where(fast > 0, 0.0, beyond)
            steps = jnp.where(whole_lanes == TILE - 1, last, sums[n])
            earlier = jnp.where(whole_lanes == 0, before, lookup(steps, preceding))
            shadow = (steps - earlier) * (jnp.abs(fast) * proj_scale)
            turned = lookup(shadow, (whole_lanes - shift_ref[a, tile]) & (TILE - 1))
            out_ref[a, tile, group * 8 : group * 8 + 8, :] = turned
        return carry

    lax.fori_loop(0, slow_ref.shape[0], one_angle, jnp.int32(0))


def project(lines, table, shift):
    row_step, col_step, steep = table
    slow = jnp.where(steep == 0, row_step, col_step)
    fast = jnp.where(steep == 0, col_step, row_step)
    slices = lines.shape[2]
    across = lines.shape[3] // TILE
    spot = jnp.arange(TILE, dtype=jnp.int32)
    gap = spot[None, :] - spot[:, None]
    prefix = jnp.concatenate([gap >= 0, jnp.maximum(gap, 0)], axis=1).astype(jnp.bfloat16)
    smem = pl.BlockSpec(memory_space=pltpu.SMEM)
    vmem = pl.BlockSpec(memory_space=pltpu.VMEM)
    held = pltpu.VMEM((2, TILE, across * slices // 8, 8, TILE), jnp.float32)
    return pl.pallas_call(
        forward_kernel,
        out_shape=jax.ShapeDtypeStruct((ANGLES, across, slices, TILE), jnp.float32),
        in_specs=[smem, smem, smem, smem, vmem, vmem],
        out_specs=vmem,
        scratch_shapes=[held, held],
        compiler_params=pltpu.CompilerParams(vmem_limit_bytes=48 << 20),
        name="project",
    )(slow, fast, steep, shift, lines, prefix)


def backward_kernel(
    row_ref,
    col_ref,
    shift_ref,
    shadow_ref,
    x_ref,
    out_ref,
    row_edge_ref,
    col_edge_ref,
    value_ref,
    step_ref,
    base_ref,
):
    slices = x_ref.shape[1]
    across = x_ref.shape[2] // TILE
    angles = shadow_ref.shape[0]
    parts = pieces(slices, across)
    centre = (TILE - 1) / 2.0
    whole_lanes = lax.broadcasted_iota(jnp.int32, (8, TILE), 1)
    lanes = whole_lanes.astype(jnp.float32) - centre
    scale = relaxation * proj_scale
    for a in range(angles):
        base_ref[a] = TILE / 2.0 - 0.5 + lanes * col_ref[a]
        for n, (tile, group) in enumerate(parts):
            value = shadow_ref[a, tile, group * 8 : group * 8 + 8, :].astype(jnp.float32) * scale
            value = lookup(value, (whole_lanes + shift_ref[a, tile]) & (TILE - 1))
            value_ref[a, n] = value
            step_ref[a, n] = jnp.roll(value, -1, axis=1) - value

    def one_row(u, carry):
        place = u.astype(jnp.float32) - centre
        sums = [
            x_ref[u, g * 8 : g * 8 + 8, t * TILE : (t + 1) * TILE].astype(jnp.float32)
            for t, g in parts
        ]
        for a in range(angles):
            z = base_ref[a] + place * row_ref[a]
            z = jnp.minimum(jnp.maximum(z, 0.0), TILE - 1.00001)
            whole = jnp.floor(z)
            part = z - whole
            index = whole.astype(jnp.int32)
            for n in range(len(parts)):
                sums[n] = sums[n] + (
                    lookup(value_ref[a, n], index) + part * lookup(step_ref[a, n], index)
                )
        for n, (t, g) in enumerate(parts):
            out_ref[u, g * 8 : g * 8 + 8, t * TILE : (t + 1) * TILE] = sums[n]
        offset = lax.rem(u, PACK) * TV_STEPS
        inside = (whole_lanes >= offset) & (whole_lanes < offset + TV_STEPS)
        for n, (t, g) in enumerate(parts):
            for side, tile, start in ((0, 0, 0), (1, across - 1, TILE - TV_STEPS)):
                if t == tile:
                    moved = lookup(sums[n], (whole_lanes + (start - offset)) & (TILE - 1))
                    spot = (side, u // PACK, slice(g * 8, g * 8 + 8))
                    col_edge_ref[spot] = jnp.where(inside, moved, col_edge_ref[spot])
        return carry

    col_edge_ref[...] = jnp.zeros(col_edge_ref.shape, jnp.float32)
    lax.fori_loop(0, TILE, one_row, jnp.int32(0))
    row_edge_ref[0] = out_ref[0:TV_STEPS]
    row_edge_ref[1] = out_ref[TILE - TV_STEPS : TILE]


def back_project(shadows, rows, table, shift):
    row_step, col_step, steep = table
    angles, across, slices, unused = shadows.shape
    smem = pl.BlockSpec(memory_space=pltpu.SMEM)
    vmem = pl.BlockSpec(memory_space=pltpu.VMEM)
    parts = across * slices // 8
    return pl.pallas_call(
        backward_kernel,
        out_shape=[
            jax.ShapeDtypeStruct(rows.shape, jnp.float32),
            jax.ShapeDtypeStruct((2, TV_STEPS) + rows.shape[1:], jnp.float32),
            jax.ShapeDtypeStruct((2, TILE // PACK, slices, TILE), jnp.float32),
        ],
        in_specs=[smem, smem, smem, vmem, vmem],
        out_specs=[vmem] * 3,
        scratch_shapes=[
            pltpu.VMEM((angles, parts, 8, TILE), jnp.float32),
            pltpu.VMEM((angles, parts, 8, TILE), jnp.float32),
            pltpu.VMEM((angles, 8, TILE), jnp.float32),
        ],
        name="back_project",
    )(row_step, col_step, shift, shadows, rows)


def ramp(offset):
    is_odd = offset % 2 != 0
    nonzero = jnp.where(offset == 0, 1, offset).astype(jnp.float32)
    values = jnp.where(is_odd, -1.0 / (math.pi * math.pi * nonzero * nonzero), 0.0)
    values = jnp.where(offset == 0, 0.25, values)
    return jnp.where(jnp.abs(offset) < TILE, values, 0.0)


MESH = pl.DeviceIdType.MESH


def exchange_kernel(
    partial_ref,
    target_ref,
    measured_ref,
    weight_ref,
    ramp_ref,
    out_ref,
    tiles,
    outgoing,
    incoming,
    residual,
    filtered,
    windows,
    landed,
    tile_sems,
    sum_sems,
    edge_sems,
    filter_sems,
    window_sems,
):
    row_count = lax.axis_size("row")
    col_count = lax.axis_size("col")
    row = lax.axis_index("row")
    col = lax.axis_index("col")
    here = measured_ref.shape[0]

    def send(src, dst, sems, k, to_row, to_col):
        return pltpu.make_async_remote_copy(
            src_ref=src,
            dst_ref=dst,
            send_sem=sems.at[0, k],
            recv_sem=sems.at[1, k],
            device_id=(to_row, to_col),
            device_id_type=MESH,
        )

    barrier = pltpu.get_barrier_semaphore()
    for k in range(1, col_count):
        pl.semaphore_signal(
            barrier, inc=1, device_id=(row, lax.rem(col + k, col_count)), device_id_type=MESH
        )
    for k in range(1, row_count):
        pl.semaphore_signal(
            barrier, inc=1, device_id=(lax.rem(row + k, row_count), col), device_id_type=MESH
        )
    pl.semaphore_wait(barrier, col_count + row_count - 2)

    copies = []
    for k in range(1, col_count):
        peer = lax.rem(col + k, col_count)
        copies.append(
            send(partial_ref.at[peer], tiles.at[col], tile_sems, k, row, peer)
        )
        copies[-1].start()
    tiles[col] = partial_ref[col]
    for k in range(1, col_count):
        copies[k - 1].wait_recv()

    def summed(block):
        chosen = jnp.where(target_ref[...] == block, tiles[...], 0.0)
        return jnp.sum(jnp.sum(chosen, axis=2), axis=0)

    sums = []
    for k in range(1, row_count):
        peer = lax.rem(row + k, row_count)
        outgoing[k] = summed(peer)
        sums.append(send(outgoing.at[k], incoming.at[k], sum_sems, k, peer, col))
        sums[-1].start()
    total = summed(row)
    for k in range(1, row_count):
        sums[k - 1].wait_recv()
        total = total + incoming[k]
    residual[1] = weight_ref[...] * (measured_ref[...] - total)

    before = send(residual.at[1], residual.at[2], edge_sems, 0, row - 1, col)
    after = send(residual.at[1], residual.at[0], edge_sems, 1, row + 1, col)

    @pl.when(row > 0)
    def _():
        before.start()

    @pl.when(row < row_count - 1)
    def _():
        after.start()

    @pl.when(row == 0)
    def _():
        residual[0] = jnp.zeros(residual.shape[1:], jnp.float32)

    @pl.when(row == row_count - 1)
    def _():
        residual[2] = jnp.zeros(residual.shape[1:], jnp.float32)

    def ramped(n):
        flat = residual[n].reshape(-1, TILE)
        return jnp.dot(
            flat,
            ramp_ref[n],
            precision=lax.Precision.HIGHEST,
            preferred_element_type=jnp.float32,
        )

    result = ramped(1)

    @pl.when(row > 0)
    def _():
        after.wait_recv()

    @pl.when(row < row_count - 1)
    def _():
        before.wait_recv()

    result = result + ramped(0) + ramped(2)
    filtered[row] = result.astype(jnp.bfloat16).reshape(filtered.shape[1:])

    gathers = []
    for k in range(1, row_count):
        peer = lax.rem(row + k, row_count)
        gathers.append(send(filtered.at[row], filtered.at[row], filter_sems, k, peer, col))
        gathers[-1].start()
    for k in range(1, row_count):
        source = lax.rem(row + row_count - k, row_count)
        send(
            filtered.at[source], filtered.at[source], filter_sems, k, source, col
        ).wait_recv()

    def window(peer):
        target = target_ref[peer]
        value = jnp.zeros(target.shape, jnp.float32)
        for block in range(row_count):
            piece = filtered[block].astype(jnp.float32)[:, None]
            value = jnp.where(target == block, piece, value)
        return value.astype(jnp.bfloat16)

    moves = []
    for k in range(1, col_count):
        peer = lax.rem(col + k, col_count)
        windows[k] = window(peer)
        moves.append(send(windows.at[k], landed.at[col], window_sems, k, row, peer))
        moves[-1].start()
    landed[col] = window(col)
    for move in moves:
        move.wait_recv()
    out_ref[...] = landed[...]

    for copy in copies + sums + gathers + moves:
        copy.wait_send()

    @pl.when(row > 0)
    def _():
        before.wait_send()

    @pl.when(row < row_count - 1)
    def _():
        after.wait_send()


def exchange(partial_value, target, measured, ray_weight):
    row_count = lax.axis_size("row")
    col_count = lax.axis_size("col")
    angles, across, slices, unused = partial_value.shape
    here = angles // col_count
    in_bins = jnp.arange(TILE, dtype=jnp.int32)
    ramps = jnp.stack(
        [ramp(in_bins[None, :] - in_bins[:, None] - n * TILE) for n in (-1, 0, 1)]
    )
    shape = (col_count, here, across, slices, TILE)
    dma = pltpu.SemaphoreType.DMA
    vmem = pl.BlockSpec(memory_space=pltpu.VMEM)
    target = jnp.broadcast_to(target[:, :, :, None, :], shape)
    block = (here, slices, TILE)
    result = pl.pallas_call(
        exchange_kernel,
        out_shape=jax.ShapeDtypeStruct(shape, jnp.bfloat16),
        in_specs=[vmem] * 5,
        out_specs=vmem,
        scratch_shapes=[
            pltpu.VMEM(shape, jnp.float32),
            pltpu.VMEM((row_count,) + block, jnp.float32),
            pltpu.VMEM((row_count,) + block, jnp.float32),
            pltpu.VMEM((3,) + block, jnp.float32),
            pltpu.VMEM((row_count,) + block, jnp.bfloat16),
            pltpu.VMEM(shape, jnp.bfloat16),
            pltpu.VMEM(shape, jnp.bfloat16),
            dma((2, col_count)),
            dma((2, row_count)),
            dma((2, 2)),
            dma((2, row_count)),
            dma((2, col_count)),
        ],
        compiler_params=pltpu.CompilerParams(collective_id=0, has_side_effects=True),
        name="exchange",
    )(
        partial_value.reshape(shape),
        target,
        measured.reshape(block),
        ray_weight.reshape(here, 1, TILE),
        ramps,
    )
    return result.reshape(partial_value.shape)


def edges_kernel(row_edge, col_edge, row_out, col_out, row_halo, col_halo, sems):
    row_count = lax.axis_size("row")
    col_count = lax.axis_size("col")
    row = lax.axis_index("row")
    col = lax.axis_index("col")
    groups = col_edge.shape[1]
    row_halo[...] = jnp.zeros(row_halo.shape, jnp.float32)
    col_halo[...] = jnp.zeros(col_halo.shape, jnp.float32)
    inner = pl.ds(1, groups)
    routes = (
        (-1, 0, row_edge.at[0], row_halo.at[1]),
        (1, 0, row_edge.at[1], row_halo.at[0]),
        (0, -1, col_edge.at[0], col_halo.at[1, inner]),
        (0, 1, col_edge.at[1], col_halo.at[0, inner]),
        (-1, -1, col_edge.at[0, 0], col_halo.at[1, groups + 1]),
        (-1, 1, col_edge.at[1, 0], col_halo.at[0, groups + 1]),
        (1, -1, col_edge.at[0, groups - 1], col_halo.at[1, 0]),
        (1, 1, col_edge.at[1, groups - 1], col_halo.at[0, 0]),
    )

    def exists(down, right):
        to_row, to_col = row + down, col + right
        return (to_row >= 0) & (to_row < row_count) & (to_col >= 0) & (to_col < col_count)

    barrier = pltpu.get_barrier_semaphore()
    for down, right, src, dst in routes:

        @pl.when(exists(down, right))
        def _(down=down, right=right):
            pl.semaphore_signal(
                barrier, inc=1, device_id=(row + down, col + right), device_id_type=MESH
            )

    rows_near = jnp.where(row > 0, 1, 0) + jnp.where(row < row_count - 1, 1, 0)
    cols_near = jnp.where(col > 0, 1, 0) + jnp.where(col < col_count - 1, 1, 0)
    pl.semaphore_wait(barrier, (rows_near + 1) * (cols_near + 1) - 1)

    copies = []
    for k, (down, right, src, dst) in enumerate(routes):
        copy = pltpu.make_async_remote_copy(
            src_ref=src,
            dst_ref=dst,
            send_sem=sems.at[0, k],
            recv_sem=sems.at[1, k],
            device_id=(row + down, col + right),
            device_id_type=MESH,
        )
        copies.append((down, right, copy))
        pl.when(exists(down, right))(copy.start)
    for down, right, copy in copies:
        pl.when(exists(-down, -right))(copy.wait_recv)
    row_out[...] = row_halo[...]
    col_out[...] = col_halo[...]
    for down, right, copy in copies:
        pl.when(exists(down, right))(copy.wait_send)


def exchange_edges(row_edge, col_edge):
    vmem = pl.BlockSpec(memory_space=pltpu.VMEM)
    wide = (2, col_edge.shape[1] + 2) + col_edge.shape[2:]
    return pl.pallas_call(
        edges_kernel,
        out_shape=[
            jax.ShapeDtypeStruct(row_edge.shape, jnp.float32),
            jax.ShapeDtypeStruct(wide, jnp.float32),
        ],
        in_specs=[vmem] * 2,
        out_specs=[vmem] * 2,
        scratch_shapes=[
            pltpu.VMEM(row_edge.shape, jnp.float32),
            pltpu.VMEM(wide, jnp.float32),
            pltpu.SemaphoreType.DMA((2, 8)),
        ],
        compiler_params=pltpu.CompilerParams(collective_id=1, has_side_effects=True),
        name="exchange_edges",
    )(row_edge, col_edge)


def smooth_kernel(near_ref, x_ref, row_halo, col_halo, out_ref, y_ref):
    height, slices, width = x_ref.shape
    full = width + TILE
    lanes = lax.broadcasted_iota(jnp.int32, (slices, TILE), 1)
    lanes8 = lax.broadcasted_iota(jnp.int32, (8, TILE), 1)
    above, below = near_ref[0] > 0, near_ref[1] > 0
    spot = lax.broadcasted_iota(jnp.int32, (slices, full), 1)
    kept = (
        (spot < width)
        | ((spot < width + TV_STEPS) & (near_ref[3] > 0))
        | ((spot >= full - TV_STEPS) & (near_ref[2] > 0))
    )
    y_ref[0:TV_STEPS, :, 0:width] = row_halo[0]
    y_ref[TV_STEPS + height :, :, 0:width] = row_halo[1]

    def fill(w, carry):
        place = w + PACK - TV_STEPS
        group = place // PACK
        offset = lax.rem(place, PACK) * TV_STEPS
        for g in range(slices // 8):
            span = slice(g * 8, g * 8 + 8)
            left = lookup(
                col_halo[0, group, span], (lanes8 + (TV_STEPS + offset)) & (TILE - 1)
            )
            right = lookup(col_halo[1, group, span], (lanes8 + offset) & (TILE - 1))
            y_ref[w, span, width:] = jnp.where(
                lanes8 >= TILE - TV_STEPS, left, jnp.where(lanes8 < TV_STEPS, right, 0.0)
            )
        return carry

    lax.fori_loop(0, height + 2 * TV_STEPS, fill, jnp.int32(0))

    def copy(u, carry):
        y_ref[u + TV_STEPS, :, 0:width] = x_ref[u]
        return carry

    lax.fori_loop(0, height, copy, jnp.int32(0))

    def flows(here, after):
        down = after - here
        across = pltpu.roll(here, full - 1, 1) - here
        scale = lax.rsqrt(smoothing * smoothing + down * down + across * across)
        return down * scale, across * scale

    for step in range(TV_STEPS):
        first = y_ref[step]
        second = y_ref[step + 1]
        flow, unused = flows(first, second)

        def one_row(w, carry, step=step):
            here, flow_above = carry
            after = y_ref[w + 1]
            flow_down, flow_right = flows(here, after)
            gradient = flow_above - flow_down + pltpu.roll(flow_right, 1, 1) - flow_right
            value = here - descent_step * gradient
            if step == TV_STEPS - 1:
                out_ref[w - TV_STEPS] = value[:, 0:width]
            else:
                inside = ((w >= TV_STEPS) | above) & ((w < height + TV_STEPS) | below)
                value = jnp.where(kept, value, 0.0)
                y_ref[w] = value * jnp.where(inside, 1.0, 0.0)
            return after, flow_down

        lax.fori_loop(
            step + 1, height + 2 * TV_STEPS - 1 - step, one_row, (second, flow), unroll=2
        )


def smooth(x, row_halo, col_halo, near):
    height, slices, width = x.shape
    vmem = pl.BlockSpec(memory_space=pltpu.VMEM)
    return pl.pallas_call(
        smooth_kernel,
        out_shape=jax.ShapeDtypeStruct(x.shape, jnp.float32),
        in_specs=[pl.BlockSpec(memory_space=pltpu.SMEM)] + [vmem] * 3,
        out_specs=vmem,
        scratch_shapes=[pltpu.VMEM((height + 2 * TV_STEPS, slices, width + TILE), jnp.float32)],
        compiler_params=pltpu.CompilerParams(vmem_limit_bytes=48 << 20),
        name="smooth",
    )(near, x, row_halo, col_halo)


def local(current_image, measured, ray_weight, angle_ids, shadow_start):
    row_index = lax.axis_index("row")
    col_index = lax.axis_index("col")
    row_count = lax.axis_size("row")
    col_count = lax.axis_size("col")
    slices = current_image.shape[0]
    local_width = current_image.shape[2]
    across = local_width // TILE
    angles_here = ANGLES // col_count
    table = angle_table(angle_ids)
    rows = current_image.transpose(1, 0, 2)
    rounded = current_image.astype(jnp.bfloat16)
    columns = rounded.reshape(slices, TILE, across, TILE).transpose(3, 0, 2, 1)
    lines = jnp.stack([rounded.transpose(1, 0, 2), columns.reshape(TILE, slices, local_width)])
    row_starts = shadow_start[row_index]
    own_starts = lax.dynamic_slice_in_dim(row_starts, col_index * across, across, 0)

    shift = own_starts.T % TILE
    partial_value = project(lines, table, shift)
    wanted = lax.dynamic_slice_in_dim(row_starts, col_index * angles_here, angles_here, 1)
    lane = jnp.arange(TILE, dtype=jnp.int32)
    target = wanted[:, :, None] // TILE + (lane < wanted[:, :, None] % TILE)
    target = target.reshape(col_count, across, angles_here, TILE).transpose(0, 2, 1, 3)
    shadows = exchange(partial_value, target.astype(jnp.int32), measured, ray_weight)
    current, row_edge, col_edge = back_project(shadows, rows, table, shift)
    row_halo, col_halo = exchange_edges(row_edge, col_edge)
    near = jnp.stack(
        [row_index > 0, row_index < row_count - 1, col_index > 0, col_index < col_count - 1]
    ).astype(jnp.int32)
    current = smooth(current, row_halo, col_halo, near).transpose(1, 0, 2)
    return current


def solution(mesh):
    return jax.shard_map(
        local,
        mesh=mesh,
        in_specs=(
            P(None, "row", "col"),
            P("col", "row", None, None),
            P("col", "row", None),
            P(),
            P(),
        ),
        out_specs=P(None, "row", "col"),
        check_vma=False,
    )
```

```python
import math

import jax
import jax.numpy as jnp
from jax import lax
from jax.experimental import pallas as pl
from jax.experimental.pallas import tpu as pltpu
from jax.sharding import PartitionSpec as P

TILE = 128
ANGLES = 16
ALL_ANGLES = 256
TV_STEPS = 4
PACK = TILE // TV_STEPS


inverse_root = 0.7071067811865476
proj_scale = 0.03125
relaxation = 8.0
smoothing = 0.25
descent_step = 0.05


def angle_table(angle_ids):
    radians = angle_ids.astype(jnp.float32) * (math.pi / ALL_ANGLES)
    row_step = jnp.cos(radians) * inverse_root
    col_step = jnp.sin(radians) * inverse_root
    steep = jnp.where(jnp.abs(col_step) >= jnp.abs(row_step), 0, 1).astype(jnp.int32)
    return row_step, col_step, steep


def lookup(table, index):
    return jnp.take_along_axis(table, index, axis=1, mode="promise_in_bounds")


def pieces(slices, across):
    return [(t, g) for t in range(across) for g in range(slices // 8)]


LINES = 8


def forward_kernel(
    slow_ref, fast_ref, steep_ref, shift_ref, x_ref, prefix_ref, out_ref, once_ref, twice_ref
):
    slices = x_ref.shape[2]
    across = x_ref.shape[3] // TILE
    groups = slices // 8
    count = across * groups
    centre = (TILE - 1) / 2.0
    whole_lanes = lax.broadcasted_iota(jnp.int32, (8, TILE), 1)
    lanes = whole_lanes.astype(jnp.float32)
    following = (whole_lanes + 1) & (TILE - 1)
    preceding = (whole_lanes - 1) & (TILE - 1)

    def fill(block, carry):
        at = pl.multiple_of(block * LINES, LINES)
        for way in range(2):
            for tile in range(across):
                flat = x_ref[way, pl.ds(at, LINES), :, tile * TILE : (tile + 1) * TILE]
                both = jnp.dot(
                    flat.reshape(LINES * slices, TILE),
                    prefix_ref[...],
                    preferred_element_type=jnp.float32,
                ).reshape(LINES, groups, 8, 2 * TILE)
                span = slice(tile * groups, (tile + 1) * groups)
                once_ref[way, pl.ds(at, LINES), span] = both[..., :TILE]
                twice_ref[way, pl.ds(at, LINES), span] = both[..., TILE:]
        return carry

    lax.fori_loop(0, TILE // LINES, fill, jnp.int32(0))
    zero = jnp.zeros((8, TILE), jnp.float32)

    def add_line(line, sums):
        return tuple(sums[n] + once_ref[0, line, n] for n in range(count))

    totals = lax.fori_loop(0, TILE, add_line, (zero,) * count)
    totals = [lookup(t, jnp.full((8, TILE), TILE - 1, jnp.int32)) for t in totals]

    def one_angle(a, carry):
        slow = slow_ref[a]
        fast = jnp.full((8, TILE), fast_ref[a], jnp.float32)
        steep = steep_ref[a]
        inverse = 1.0 / fast
        base = (lanes + (0.5 - TILE / 2.0)) * inverse + centre
        tilt = slow * inverse

        def some_lines(block, sums):
            here = [zero] * count
            for k in range(LINES):
                line = block * LINES + k
                q = jnp.maximum(base - (line.astype(jnp.float32) - centre) * tilt, 0.0)
                whole = jnp.minimum(jnp.floor(q), TILE - 1.0)
                part = q - whole
                index = whole.astype(jnp.int32)
                first = [lookup(once_ref[steep, line, n], index) for n in range(count)]
                second = [lookup(twice_ref[steep, line, n], index) for n in range(count)]
                for n in range(count):
                    here[n] = here[n] + (second[n] + part * first[n])
            return tuple(
                sums[n] + (lookup(here[n], following) - here[n]) for n in range(count)
            )

        sums = lax.fori_loop(0, TILE // LINES, some_lines, (zero,) * count, unroll=4)
        sent = []
        for n in range(count):
            tile = n // groups
            beyond = totals[n] * inverse
            last = jnp.where(fast > 0, beyond, 0.0)
            before = jnp.where(fast > 0, 0.0, beyond)
            steps = jnp.where(whole_lanes == TILE - 1, last, sums[n])
            earlier = jnp.where(whole_lanes == 0, before, lookup(steps, preceding))
            shadow = (steps - earlier) * (jnp.abs(fast) * proj_scale)
            turned = lookup(shadow, (whole_lanes - shift_ref[a, tile]) & (TILE - 1))
            sent.append(turned)
        for tile in range(across):
            both = jnp.concatenate(sent[tile * groups : (tile + 1) * groups], axis=0)
            out_ref[a, tile] = both.astype(out_ref.dtype)
        return carry

    lax.fori_loop(0, slow_ref.shape[0], one_angle, jnp.int32(0))


def project(lines, table, shift):
    row_step, col_step, steep = table
    slow = jnp.where(steep == 0, row_step, col_step)
    fast = jnp.where(steep == 0, col_step, row_step)
    slices = lines.shape[2]
    across = lines.shape[3] // TILE
    spot = jnp.arange(TILE, dtype=jnp.int32)
    gap = spot[None, :] - spot[:, None]
    prefix = jnp.concatenate([gap >= 0, jnp.maximum(gap, 0)], axis=1).astype(jnp.bfloat16)
    smem = pl.BlockSpec(memory_space=pltpu.SMEM)
    vmem = pl.BlockSpec(memory_space=pltpu.VMEM)
    held = pltpu.VMEM((2, TILE, across * slices // 8, 8, TILE), jnp.float32)
    return pl.pallas_call(
        forward_kernel,
        out_shape=jax.ShapeDtypeStruct((ANGLES, across, slices, TILE), jnp.bfloat16),
        in_specs=[smem, smem, smem, smem, vmem, vmem],
        out_specs=vmem,
        scratch_shapes=[held, held],
        compiler_params=pltpu.CompilerParams(vmem_limit_bytes=48 << 20),
        name="project",
    )(slow, fast, steep, shift, lines, prefix)


def backward_kernel(
    row_ref,
    col_ref,
    shift_ref,
    shadow_ref,
    x_ref,
    out_ref,
    row_edge_ref,
    col_edge_ref,
    value_ref,
    step_ref,
    base_ref,
):
    slices = x_ref.shape[1]
    across = x_ref.shape[2] // TILE
    angles = shadow_ref.shape[0]
    parts = pieces(slices, across)
    centre = (TILE - 1) / 2.0
    whole_lanes = lax.broadcasted_iota(jnp.int32, (8, TILE), 1)
    lanes = whole_lanes.astype(jnp.float32) - centre
    scale = relaxation * proj_scale
    for a in range(angles):
        base_ref[a] = TILE / 2.0 - 0.5 + lanes * col_ref[a]
        for n, (tile, group) in enumerate(parts):
            value = shadow_ref[a, tile, group * 8 : group * 8 + 8, :].astype(jnp.float32) * scale
            value = lookup(value, (whole_lanes + shift_ref[a, tile]) & (TILE - 1))
            value_ref[a, n] = value
            step_ref[a, n] = jnp.roll(value, -1, axis=1) - value

    def one_row(u, carry):
        place = u.astype(jnp.float32) - centre
        sums = [
            x_ref[u, g * 8 : g * 8 + 8, t * TILE : (t + 1) * TILE].astype(jnp.float32)
            for t, g in parts
        ]
        for a in range(angles):
            z = base_ref[a] + place * row_ref[a]
            z = jnp.minimum(jnp.maximum(z, 0.0), TILE - 1.00001)
            whole = jnp.floor(z)
            part = z - whole
            index = whole.astype(jnp.int32)
            for n in range(len(parts)):
                sums[n] = sums[n] + (
                    lookup(value_ref[a, n], index) + part * lookup(step_ref[a, n], index)
                )
        for n, (t, g) in enumerate(parts):
            out_ref[u, g * 8 : g * 8 + 8, t * TILE : (t + 1) * TILE] = sums[n]
        return carry

    lax.fori_loop(0, TILE, one_row, jnp.int32(0))

    def pack(block, carry):
        for side, tile, start in ((0, 0, 0), (1, across - 1, TILE - TV_STEPS)):
            for g in range(slices // 8):
                span = slice(g * 8, g * 8 + 8)
                packed = jnp.zeros((8, TILE), jnp.float32)
                for r in range(PACK):
                    offset = r * TV_STEPS
                    inside = (whole_lanes >= offset) & (whole_lanes < offset + TV_STEPS)
                    row = out_ref[block * PACK + r, span, tile * TILE : (tile + 1) * TILE]
                    moved = lookup(row, (whole_lanes + (start - offset)) & (TILE - 1))
                    packed = jnp.where(inside, moved, packed)
                col_edge_ref[side, block, span] = packed
        return carry

    lax.fori_loop(0, TILE // PACK, pack, jnp.int32(0))
    row_edge_ref[0] = out_ref[0:TV_STEPS]
    row_edge_ref[1] = out_ref[TILE - TV_STEPS : TILE]


def back_project(shadows, rows, table, shift):
    row_step, col_step, steep = table
    angles, across, slices, unused = shadows.shape
    smem = pl.BlockSpec(memory_space=pltpu.SMEM)
    vmem = pl.BlockSpec(memory_space=pltpu.VMEM)
    parts = across * slices // 8
    return pl.pallas_call(
        backward_kernel,
        out_shape=[
            jax.ShapeDtypeStruct(rows.shape, jnp.float32),
            jax.ShapeDtypeStruct((2, TV_STEPS) + rows.shape[1:], jnp.float32),
            jax.ShapeDtypeStruct((2, TILE // PACK, slices, TILE), jnp.float32),
        ],
        in_specs=[smem, smem, smem, vmem, vmem],
        out_specs=[vmem] * 3,
        scratch_shapes=[
            pltpu.VMEM((angles, parts, 8, TILE), jnp.float32),
            pltpu.VMEM((angles, parts, 8, TILE), jnp.float32),
            pltpu.VMEM((angles, 8, TILE), jnp.float32),
        ],
        name="back_project",
    )(row_step, col_step, shift, shadows, rows)


def ramp(offset):
    is_odd = offset % 2 != 0
    nonzero = jnp.where(offset == 0, 1, offset).astype(jnp.float32)
    values = jnp.where(is_odd, -1.0 / (math.pi * math.pi * nonzero * nonzero), 0.0)
    values = jnp.where(offset == 0, 0.25, values)
    return jnp.where(jnp.abs(offset) < TILE, values, 0.0)


MESH = pl.DeviceIdType.MESH


def exchange_kernel(
    partial_ref,
    target_ref,
    measured_ref,
    weight_ref,
    ramp_ref,
    out_ref,
    tiles,
    outgoing,
    incoming,
    residual,
    filtered,
    windows,
    landed,
    tile_sems,
    sum_sems,
    edge_sems,
    filter_sems,
    window_sems,
):
    row_count = lax.axis_size("row")
    col_count = lax.axis_size("col")
    row = lax.axis_index("row")
    col = lax.axis_index("col")
    here = measured_ref.shape[0]

    def send(src, dst, sems, k, to_row, to_col):
        return pltpu.make_async_remote_copy(
            src_ref=src,
            dst_ref=dst,
            send_sem=sems.at[0, k],
            recv_sem=sems.at[1, k],
            device_id=(to_row, to_col),
            device_id_type=MESH,
        )

    barrier = pltpu.get_barrier_semaphore()
    for k in range(1, col_count):
        pl.semaphore_signal(
            barrier, inc=1, device_id=(row, lax.rem(col + k, col_count)), device_id_type=MESH
        )
    for k in range(1, row_count):
        pl.semaphore_signal(
            barrier, inc=1, device_id=(lax.rem(row + k, row_count), col), device_id_type=MESH
        )
    pl.semaphore_wait(barrier, col_count + row_count - 2)

    copies = []
    for k in range(1, col_count):
        peer = lax.rem(col + k, col_count)
        copies.append(
            send(partial_ref.at[peer], tiles.at[col], tile_sems, k, row, peer)
        )
        copies[-1].start()
    tiles[col] = partial_ref[col]
    for k in range(1, col_count):
        copies[k - 1].wait_recv()

    def summed(block):
        chosen = jnp.where(target_ref[...] == block, tiles[...].astype(jnp.float32), 0.0)
        return jnp.sum(jnp.sum(chosen, axis=2), axis=0)

    sums = []
    for k in range(1, row_count):
        peer = lax.rem(row + k, row_count)
        outgoing[k] = summed(peer).astype(outgoing.dtype)
        sums.append(send(outgoing.at[k], incoming.at[k], sum_sems, k, peer, col))
        sums[-1].start()
    total = summed(row)
    for k in range(1, row_count):
        sums[k - 1].wait_recv()
        total = total + incoming[k].astype(jnp.float32)
    residual[1] = weight_ref[...] * (measured_ref[...] - total)

    before = send(residual.at[1], residual.at[2], edge_sems, 0, row - 1, col)
    after = send(residual.at[1], residual.at[0], edge_sems, 1, row + 1, col)

    @pl.when(row > 0)
    def _():
        before.start()

    @pl.when(row < row_count - 1)
    def _():
        after.start()

    @pl.when(row == 0)
    def _():
        residual[0] = jnp.zeros(residual.shape[1:], jnp.float32)

    @pl.when(row == row_count - 1)
    def _():
        residual[2] = jnp.zeros(residual.shape[1:], jnp.float32)

    def ramped(n):
        flat = residual[n].reshape(-1, TILE)
        return jnp.dot(
            flat,
            ramp_ref[n],
            precision=lax.Precision.HIGHEST,
            preferred_element_type=jnp.float32,
        )

    result = ramped(1)

    @pl.when(row > 0)
    def _():
        after.wait_recv()

    @pl.when(row < row_count - 1)
    def _():
        before.wait_recv()

    result = result + ramped(0) + ramped(2)
    filtered[row] = result.astype(jnp.bfloat16).reshape(filtered.shape[1:])

    gathers = []
    for k in range(1, row_count):
        peer = lax.rem(row + k, row_count)
        gathers.append(send(filtered.at[row], filtered.at[row], filter_sems, k, peer, col))
        gathers[-1].start()
    for k in range(1, row_count):
        source = lax.rem(row + row_count - k, row_count)
        send(
            filtered.at[source], filtered.at[source], filter_sems, k, source, col
        ).wait_recv()

    def window(peer):
        target = target_ref[peer]
        value = jnp.zeros(target.shape, jnp.float32)
        for block in range(row_count):
            piece = filtered[block].astype(jnp.float32)[:, None]
            value = jnp.where(target == block, piece, value)
        return value.astype(jnp.bfloat16)

    moves = []
    for k in range(1, col_count):
        peer = lax.rem(col + k, col_count)
        windows[k] = window(peer)
        moves.append(send(windows.at[k], landed.at[col], window_sems, k, row, peer))
        moves[-1].start()
    landed[col] = window(col)
    for move in moves:
        move.wait_recv()
    out_ref[...] = landed[...]

    for copy in copies + sums + gathers + moves:
        copy.wait_send()

    @pl.when(row > 0)
    def _():
        before.wait_send()

    @pl.when(row < row_count - 1)
    def _():
        after.wait_send()


def exchange(partial_value, target, measured, ray_weight):
    row_count = lax.axis_size("row")
    col_count = lax.axis_size("col")
    angles, across, slices, unused = partial_value.shape
    here = angles // col_count
    in_bins = jnp.arange(TILE, dtype=jnp.int32)
    ramps = jnp.stack(
        [ramp(in_bins[None, :] - in_bins[:, None] - n * TILE) for n in (-1, 0, 1)]
    )
    shape = (col_count, here, across, slices, TILE)
    dma = pltpu.SemaphoreType.DMA
    vmem = pl.BlockSpec(memory_space=pltpu.VMEM)
    target = jnp.broadcast_to(target[:, :, :, None, :], shape)
    block = (here, slices, TILE)
    result = pl.pallas_call(
        exchange_kernel,
        out_shape=jax.ShapeDtypeStruct(shape, jnp.bfloat16),
        in_specs=[vmem] * 5,
        out_specs=vmem,
        scratch_shapes=[
            pltpu.VMEM(shape, jnp.bfloat16),
            pltpu.VMEM((row_count,) + block, jnp.bfloat16),
            pltpu.VMEM((row_count,) + block, jnp.bfloat16),
            pltpu.VMEM((3,) + block, jnp.float32),
            pltpu.VMEM((row_count,) + block, jnp.bfloat16),
            pltpu.VMEM(shape, jnp.bfloat16),
            pltpu.VMEM(shape, jnp.bfloat16),
            dma((2, col_count)),
            dma((2, row_count)),
            dma((2, 2)),
            dma((2, row_count)),
            dma((2, col_count)),
        ],
        compiler_params=pltpu.CompilerParams(collective_id=0, has_side_effects=True),
        name="exchange",
    )(
        partial_value.reshape(shape),
        target,
        measured.reshape(block),
        ray_weight.reshape(here, 1, TILE),
        ramps,
    )
    return result.reshape(partial_value.shape)


def edges_kernel(row_edge, col_edge, row_out, col_out, row_halo, col_halo, sems):
    row_count = lax.axis_size("row")
    col_count = lax.axis_size("col")
    row = lax.axis_index("row")
    col = lax.axis_index("col")
    groups = col_edge.shape[1]
    row_halo[...] = jnp.zeros(row_halo.shape, jnp.float32)
    col_halo[...] = jnp.zeros(col_halo.shape, jnp.float32)
    inner = pl.ds(1, groups)
    routes = (
        (-1, 0, row_edge.at[0], row_halo.at[1]),
        (1, 0, row_edge.at[1], row_halo.at[0]),
        (0, -1, col_edge.at[0], col_halo.at[1, inner]),
        (0, 1, col_edge.at[1], col_halo.at[0, inner]),
        (-1, -1, col_edge.at[0, 0], col_halo.at[1, groups + 1]),
        (-1, 1, col_edge.at[1, 0], col_halo.at[0, groups + 1]),
        (1, -1, col_edge.at[0, groups - 1], col_halo.at[1, 0]),
        (1, 1, col_edge.at[1, groups - 1], col_halo.at[0, 0]),
    )

    def exists(down, right):
        to_row, to_col = row + down, col + right
        return (to_row >= 0) & (to_row < row_count) & (to_col >= 0) & (to_col < col_count)

    barrier = pltpu.get_barrier_semaphore()
    for down, right, src, dst in routes:

        @pl.when(exists(down, right))
        def _(down=down, right=right):
            pl.semaphore_signal(
                barrier, inc=1, device_id=(row + down, col + right), device_id_type=MESH
            )

    rows_near = jnp.where(row > 0, 1, 0) + jnp.where(row < row_count - 1, 1, 0)
    cols_near = jnp.where(col > 0, 1, 0) + jnp.where(col < col_count - 1, 1, 0)
    pl.semaphore_wait(barrier, (rows_near + 1) * (cols_near + 1) - 1)

    copies = []
    for k, (down, right, src, dst) in enumerate(routes):
        copy = pltpu.make_async_remote_copy(
            src_ref=src,
            dst_ref=dst,
            send_sem=sems.at[0, k],
            recv_sem=sems.at[1, k],
            device_id=(row + down, col + right),
            device_id_type=MESH,
        )
        copies.append((down, right, copy))
        pl.when(exists(down, right))(copy.start)
    for down, right, copy in copies:
        pl.when(exists(-down, -right))(copy.wait_recv)
    row_out[...] = row_halo[...]
    col_out[...] = col_halo[...]
    for down, right, copy in copies:
        pl.when(exists(down, right))(copy.wait_send)


def exchange_edges(row_edge, col_edge):
    vmem = pl.BlockSpec(memory_space=pltpu.VMEM)
    wide = (2, col_edge.shape[1] + 2) + col_edge.shape[2:]
    return pl.pallas_call(
        edges_kernel,
        out_shape=[
            jax.ShapeDtypeStruct(row_edge.shape, jnp.float32),
            jax.ShapeDtypeStruct(wide, jnp.float32),
        ],
        in_specs=[vmem] * 2,
        out_specs=[vmem] * 2,
        scratch_shapes=[
            pltpu.VMEM(row_edge.shape, jnp.float32),
            pltpu.VMEM(wide, jnp.float32),
            pltpu.SemaphoreType.DMA((2, 8)),
        ],
        compiler_params=pltpu.CompilerParams(collective_id=1, has_side_effects=True),
        name="exchange_edges",
    )(row_edge, col_edge)


ROWS = 8


def smooth_kernel(near_ref, x_ref, row_halo, col_halo, out_ref, y_ref):
    height, slices, width = x_ref.shape
    full = width + TILE
    lanes = lax.broadcasted_iota(jnp.int32, (slices, TILE), 1)
    lanes8 = lax.broadcasted_iota(jnp.int32, (8, TILE), 1)
    above, below = near_ref[0] > 0, near_ref[1] > 0
    spot = lax.broadcasted_iota(jnp.int32, (slices, full), 1)
    kept = (
        (spot < width)
        | ((spot < width + TV_STEPS) & (near_ref[3] > 0))
        | ((spot >= full - TV_STEPS) & (near_ref[2] > 0))
    )
    y_ref[0:TV_STEPS, :, 0:width] = row_halo[0]
    y_ref[TV_STEPS + height : 2 * TV_STEPS + height, :, 0:width] = row_halo[1]

    def fill(w, carry):
        place = w + PACK - TV_STEPS
        group = place // PACK
        offset = lax.rem(place, PACK) * TV_STEPS
        for g in range(slices // 8):
            span = slice(g * 8, g * 8 + 8)
            left = lookup(
                col_halo[0, group, span], (lanes8 + (TV_STEPS + offset)) & (TILE - 1)
            )
            right = lookup(col_halo[1, group, span], (lanes8 + offset) & (TILE - 1))
            y_ref[w, span, width:] = jnp.where(
                lanes8 >= TILE - TV_STEPS, left, jnp.where(lanes8 < TV_STEPS, right, 0.0)
            )
        return carry

    lax.fori_loop(0, height + 2 * TV_STEPS, fill, jnp.int32(0), unroll=8)
    spare = y_ref.shape[0] - height - 2 * TV_STEPS
    y_ref[height + 2 * TV_STEPS :] = jnp.zeros((spare, slices, full), jnp.float32)

    def copy(u, carry):
        y_ref[u + TV_STEPS, :, 0:width] = x_ref[u]
        return carry

    lax.fori_loop(0, height, copy, jnp.int32(0), unroll=8)

    def flows(here, after):
        down = after - here
        across = pltpu.roll(here, full - 1, 1) - here
        scale = lax.rsqrt(smoothing * smoothing + down * down + across * across)
        return down * scale, across * scale

    for step in range(TV_STEPS):
        flow = flows(y_ref[step], y_ref[step + 1])[0]

        def some_rows(block, above_flow, step=step):
            w = step + 1 + block * ROWS
            olds = [y_ref[w + k] for k in range(ROWS + 1)]
            news = []
            for k in range(ROWS):
                flow_down, flow_right = flows(olds[k], olds[k + 1])
                gradient = above_flow - flow_down + pltpu.roll(flow_right, 1, 1) - flow_right
                news.append(olds[k] - descent_step * gradient)
                above_flow = flow_down
            for k, value in enumerate(news):
                if step == TV_STEPS - 1:
                    out_ref[w + k - TV_STEPS] = value[:, 0:width]
                else:
                    row = w + k
                    inside = ((row >= TV_STEPS) | above) & ((row < height + TV_STEPS) | below)
                    y_ref[row] = jnp.where(kept, value, 0.0) * jnp.where(inside, 1.0, 0.0)
            return above_flow

        rows = height + 2 * (TV_STEPS - 1 - step)
        lax.fori_loop(0, pl.cdiv(rows, ROWS), some_rows, flow)


def smooth(x, row_halo, col_halo, near):
    height, slices, width = x.shape
    vmem = pl.BlockSpec(memory_space=pltpu.VMEM)
    return pl.pallas_call(
        smooth_kernel,
        out_shape=jax.ShapeDtypeStruct(x.shape, jnp.float32),
        in_specs=[pl.BlockSpec(memory_space=pltpu.SMEM)] + [vmem] * 3,
        out_specs=vmem,
        scratch_shapes=[pltpu.VMEM((height + 2 * TV_STEPS + ROWS, slices, width + TILE), jnp.float32)],
        compiler_params=pltpu.CompilerParams(vmem_limit_bytes=48 << 20),
        name="smooth",
    )(near, x, row_halo, col_halo)


def local(current_image, measured, ray_weight, angle_ids, shadow_start):
    row_index = lax.axis_index("row")
    col_index = lax.axis_index("col")
    row_count = lax.axis_size("row")
    col_count = lax.axis_size("col")
    slices = current_image.shape[0]
    local_width = current_image.shape[2]
    across = local_width // TILE
    angles_here = ANGLES // col_count
    table = angle_table(angle_ids)
    rows = current_image.transpose(1, 0, 2)
    rounded = current_image.astype(jnp.bfloat16)
    columns = rounded.reshape(slices, TILE, across, TILE).transpose(3, 0, 2, 1)
    lines = jnp.stack([rounded.transpose(1, 0, 2), columns.reshape(TILE, slices, local_width)])
    row_starts = shadow_start[row_index]
    own_starts = lax.dynamic_slice_in_dim(row_starts, col_index * across, across, 0)

    shift = own_starts.T % TILE
    partial_value = project(lines, table, shift)
    wanted = lax.dynamic_slice_in_dim(row_starts, col_index * angles_here, angles_here, 1)
    lane = jnp.arange(TILE, dtype=jnp.int32)
    target = wanted[:, :, None] // TILE + (lane < wanted[:, :, None] % TILE)
    target = target.reshape(col_count, across, angles_here, TILE).transpose(0, 2, 1, 3)
    shadows = exchange(partial_value, target.astype(jnp.int32), measured, ray_weight)
    current, row_edge, col_edge = back_project(shadows, rows, table, shift)
    row_halo, col_halo = exchange_edges(row_edge, col_edge)
    near = jnp.stack(
        [row_index > 0, row_index < row_count - 1, col_index > 0, col_index < col_count - 1]
    ).astype(jnp.int32)
    current = smooth(current, row_halo, col_halo, near).transpose(1, 0, 2)
    return current


def solution(mesh):
    return jax.shard_map(
        local,
        mesh=mesh,
        in_specs=(
            P(None, "row", "col"),
            P("col", "row", None, None),
            P("col", "row", None),
            P(),
            P(),
        ),
        out_specs=P(None, "row", "col"),
        check_vma=False,
    )
```

```python
import math

import jax
import jax.numpy as jnp
from jax import lax
from jax.experimental import pallas as pl
from jax.experimental.pallas import tpu as pltpu
from jax.sharding import PartitionSpec as P

TILE = 128
ANGLES = 16
ALL_ANGLES = 256
TV_STEPS = 4
PACK = TILE // TV_STEPS


inverse_root = 0.7071067811865476
proj_scale = 0.03125
relaxation = 8.0
smoothing = 0.25
descent_step = 0.05


def angle_table(angle_ids):
    radians = angle_ids.astype(jnp.float32) * (math.pi / ALL_ANGLES)
    row_step = jnp.cos(radians) * inverse_root
    col_step = jnp.sin(radians) * inverse_root
    steep = jnp.where(jnp.abs(col_step) >= jnp.abs(row_step), 0, 1).astype(jnp.int32)
    return row_step, col_step, steep


def lookup(table, index):
    return jnp.take_along_axis(table, index, axis=1, mode="promise_in_bounds")


def pieces(slices, across):
    return [(t, g) for t in range(across) for g in range(slices // 8)]


LINES = 8


def forward_kernel(
    slow_ref, fast_ref, steep_ref, shift_ref, x_ref, prefix_ref, out_ref, once_ref, twice_ref
):
    slices = x_ref.shape[2]
    across = x_ref.shape[3] // TILE
    groups = slices // 8
    count = across * groups
    centre = (TILE - 1) / 2.0
    whole_lanes = lax.broadcasted_iota(jnp.int32, (8, TILE), 1)
    lanes = whole_lanes.astype(jnp.float32)
    following = (whole_lanes + 1) & (TILE - 1)
    preceding = (whole_lanes - 1) & (TILE - 1)

    def fill(block, carry):
        at = pl.multiple_of(block * LINES, LINES)
        for way in range(2):
            for tile in range(across):
                flat = x_ref[way, pl.ds(at, LINES), :, tile * TILE : (tile + 1) * TILE]
                both = jnp.dot(
                    flat.reshape(LINES * slices, TILE),
                    prefix_ref[...],
                    preferred_element_type=jnp.float32,
                ).reshape(LINES, groups, 8, 2 * TILE)
                span = slice(tile * groups, (tile + 1) * groups)
                once_ref[way, pl.ds(at, LINES), span] = both[..., :TILE]
                twice_ref[way, pl.ds(at, LINES), span] = both[..., TILE:]
        return carry

    lax.fori_loop(0, TILE // LINES, fill, jnp.int32(0))
    zero = jnp.zeros((8, TILE), jnp.float32)

    def add_line(line, sums):
        return tuple(sums[n] + once_ref[0, line, n] for n in range(count))

    totals = lax.fori_loop(0, TILE, add_line, (zero,) * count)
    totals = [lookup(t, jnp.full((8, TILE), TILE - 1, jnp.int32)) for t in totals]

    def one_angle(a, carry):
        slow = slow_ref[a]
        fast = jnp.full((8, TILE), fast_ref[a], jnp.float32)
        steep = steep_ref[a]
        inverse = 1.0 / fast
        base = (lanes + (0.5 - TILE / 2.0)) * inverse + centre
        tilt = slow * inverse

        def some_lines(block, sums):
            here = [zero] * count
            for k in range(LINES):
                line = block * LINES + k
                q = jnp.maximum(base - (line.astype(jnp.float32) - centre) * tilt, 0.0)
                whole = jnp.minimum(jnp.floor(q), TILE - 1.0)
                part = q - whole
                index = whole.astype(jnp.int32)
                first = [lookup(once_ref[steep, line, n], index) for n in range(count)]
                second = [lookup(twice_ref[steep, line, n], index) for n in range(count)]
                for n in range(count):
                    here[n] = here[n] + (second[n] + part * first[n])
            return tuple(
                sums[n] + (lookup(here[n], following) - here[n]) for n in range(count)
            )

        sums = lax.fori_loop(0, TILE // LINES, some_lines, (zero,) * count, unroll=8)
        sent = []
        for n in range(count):
            tile = n // groups
            beyond = totals[n] * inverse
            last = jnp.where(fast > 0, beyond, 0.0)
            before = jnp.where(fast > 0, 0.0, beyond)
            steps = jnp.where(whole_lanes == TILE - 1, last, sums[n])
            earlier = jnp.where(whole_lanes == 0, before, lookup(steps, preceding))
            shadow = (steps - earlier) * (jnp.abs(fast) * proj_scale)
            turned = lookup(shadow, (whole_lanes - shift_ref[a, tile]) & (TILE - 1))
            sent.append(turned)
        for tile in range(across):
            both = jnp.concatenate(sent[tile * groups : (tile + 1) * groups], axis=0)
            out_ref[a, tile] = both.astype(out_ref.dtype)
        return carry

    lax.fori_loop(0, slow_ref.shape[0], one_angle, jnp.int32(0))


def project(lines, table, shift):
    row_step, col_step, steep = table
    slow = jnp.where(steep == 0, row_step, col_step)
    fast = jnp.where(steep == 0, col_step, row_step)
    slices = lines.shape[2]
    across = lines.shape[3] // TILE
    spot = jnp.arange(TILE, dtype=jnp.int32)
    gap = spot[None, :] - spot[:, None]
    prefix = jnp.concatenate([gap >= 0, jnp.maximum(gap, 0)], axis=1).astype(jnp.bfloat16)
    smem = pl.BlockSpec(memory_space=pltpu.SMEM)
    vmem = pl.BlockSpec(memory_space=pltpu.VMEM)
    held = pltpu.VMEM((2, TILE, across * slices // 8, 8, TILE), jnp.float32)
    return pl.pallas_call(
        forward_kernel,
        out_shape=jax.ShapeDtypeStruct((ANGLES, across, slices, TILE), jnp.bfloat16),
        in_specs=[smem, smem, smem, smem, vmem, vmem],
        out_specs=vmem,
        scratch_shapes=[held, held],
        compiler_params=pltpu.CompilerParams(vmem_limit_bytes=48 << 20),
        name="project",
    )(slow, fast, steep, shift, lines, prefix)


def backward_kernel(
    row_ref,
    col_ref,
    shift_ref,
    shadow_ref,
    x_ref,
    out_ref,
    row_edge_ref,
    col_edge_ref,
    value_ref,
    step_ref,
    base_ref,
):
    slices = x_ref.shape[1]
    across = x_ref.shape[2] // TILE
    angles = shadow_ref.shape[0]
    parts = pieces(slices, across)
    centre = (TILE - 1) / 2.0
    whole_lanes = lax.broadcasted_iota(jnp.int32, (8, TILE), 1)
    lanes = whole_lanes.astype(jnp.float32) - centre
    scale = relaxation * proj_scale
    for a in range(angles):
        base_ref[a] = TILE / 2.0 - 0.5 + lanes * col_ref[a]
        for n, (tile, group) in enumerate(parts):
            value = shadow_ref[a, tile, group * 8 : group * 8 + 8, :].astype(jnp.float32) * scale
            value = lookup(value, (whole_lanes + shift_ref[a, tile]) & (TILE - 1))
            value_ref[a, n] = value
            step_ref[a, n] = jnp.roll(value, -1, axis=1) - value

    def one_row(u, carry):
        place = u.astype(jnp.float32) - centre
        sums = [
            x_ref[u, g * 8 : g * 8 + 8, t * TILE : (t + 1) * TILE].astype(jnp.float32)
            for t, g in parts
        ]
        for a in range(angles):
            z = base_ref[a] + place * row_ref[a]
            z = jnp.minimum(jnp.maximum(z, 0.0), TILE - 1.00001)
            whole = jnp.floor(z)
            part = z - whole
            index = whole.astype(jnp.int32)
            for n in range(len(parts)):
                sums[n] = sums[n] + (
                    lookup(value_ref[a, n], index) + part * lookup(step_ref[a, n], index)
                )
        for n, (t, g) in enumerate(parts):
            out_ref[u, g * 8 : g * 8 + 8, t * TILE : (t + 1) * TILE] = sums[n]
        return carry

    lax.fori_loop(0, TILE, one_row, jnp.int32(0), unroll=2)

    def pack(block, carry):
        for side, tile, start in ((0, 0, 0), (1, across - 1, TILE - TV_STEPS)):
            for g in range(slices // 8):
                span = slice(g * 8, g * 8 + 8)
                packed = jnp.zeros((8, TILE), jnp.float32)
                for r in range(PACK):
                    offset = r * TV_STEPS
                    inside = (whole_lanes >= offset) & (whole_lanes < offset + TV_STEPS)
                    row = out_ref[block * PACK + r, span, tile * TILE : (tile + 1) * TILE]
                    moved = lookup(row, (whole_lanes + (start - offset)) & (TILE - 1))
                    packed = jnp.where(inside, moved, packed)
                col_edge_ref[side, block, span] = packed
        return carry

    lax.fori_loop(0, TILE // PACK, pack, jnp.int32(0))
    row_edge_ref[0] = out_ref[0:TV_STEPS]
    row_edge_ref[1] = out_ref[TILE - TV_STEPS : TILE]


def back_project(shadows, rows, table, shift):
    row_step, col_step, steep = table
    angles, across, slices, unused = shadows.shape
    smem = pl.BlockSpec(memory_space=pltpu.SMEM)
    vmem = pl.BlockSpec(memory_space=pltpu.VMEM)
    parts = across * slices // 8
    return pl.pallas_call(
        backward_kernel,
        out_shape=[
            jax.ShapeDtypeStruct(rows.shape, jnp.float32),
            jax.ShapeDtypeStruct((2, TV_STEPS) + rows.shape[1:], jnp.float32),
            jax.ShapeDtypeStruct((2, TILE // PACK, slices, TILE), jnp.float32),
        ],
        in_specs=[smem, smem, smem, vmem, vmem],
        out_specs=[vmem] * 3,
        scratch_shapes=[
            pltpu.VMEM((angles, parts, 8, TILE), jnp.float32),
            pltpu.VMEM((angles, parts, 8, TILE), jnp.float32),
            pltpu.VMEM((angles, 8, TILE), jnp.float32),
        ],
        name="back_project",
    )(row_step, col_step, shift, shadows, rows)


def ramp(offset):
    is_odd = offset % 2 != 0
    nonzero = jnp.where(offset == 0, 1, offset).astype(jnp.float32)
    values = jnp.where(is_odd, -1.0 / (math.pi * math.pi * nonzero * nonzero), 0.0)
    values = jnp.where(offset == 0, 0.25, values)
    return jnp.where(jnp.abs(offset) < TILE, values, 0.0)


MESH = pl.DeviceIdType.MESH


def exchange_kernel(
    partial_ref,
    target_ref,
    measured_ref,
    weight_ref,
    ramp_ref,
    out_ref,
    tiles,
    outgoing,
    incoming,
    residual,
    filtered,
    windows,
    landed,
    tile_sems,
    sum_sems,
    edge_sems,
    filter_sems,
    window_sems,
):
    row_count = lax.axis_size("row")
    col_count = lax.axis_size("col")
    row = lax.axis_index("row")
    col = lax.axis_index("col")
    here = measured_ref.shape[0]

    def send(src, dst, sems, k, to_row, to_col):
        return pltpu.make_async_remote_copy(
            src_ref=src,
            dst_ref=dst,
            send_sem=sems.at[0, k],
            recv_sem=sems.at[1, k],
            device_id=(to_row, to_col),
            device_id_type=MESH,
        )

    barrier = pltpu.get_barrier_semaphore()
    for k in range(1, col_count):
        pl.semaphore_signal(
            barrier, inc=1, device_id=(row, lax.rem(col + k, col_count)), device_id_type=MESH
        )
    for k in range(1, row_count):
        pl.semaphore_signal(
            barrier, inc=1, device_id=(lax.rem(row + k, row_count), col), device_id_type=MESH
        )
    pl.semaphore_wait(barrier, col_count + row_count - 2)

    copies = []
    for k in range(1, col_count):
        peer = lax.rem(col + k, col_count)
        copies.append(
            send(partial_ref.at[peer], tiles.at[col], tile_sems, k, row, peer)
        )
        copies[-1].start()
    tiles[col] = partial_ref[col]
    for k in range(1, col_count):
        copies[k - 1].wait_recv()

    def summed(block):
        chosen = jnp.where(target_ref[...] == block, tiles[...].astype(jnp.float32), 0.0)
        return jnp.sum(jnp.sum(chosen, axis=2), axis=0)

    sums = []
    for k in range(1, row_count):
        peer = lax.rem(row + k, row_count)
        outgoing[k] = summed(peer).astype(outgoing.dtype)
        sums.append(send(outgoing.at[k], incoming.at[k], sum_sems, k, peer, col))
        sums[-1].start()
    total = summed(row)
    for k in range(1, row_count):
        sums[k - 1].wait_recv()
        total = total + incoming[k].astype(jnp.float32)
    residual[1] = weight_ref[...] * (measured_ref[...] - total)

    before = send(residual.at[1], residual.at[2], edge_sems, 0, row - 1, col)
    after = send(residual.at[1], residual.at[0], edge_sems, 1, row + 1, col)

    @pl.when(row > 0)
    def _():
        before.start()

    @pl.when(row < row_count - 1)
    def _():
        after.start()

    @pl.when(row == 0)
    def _():
        residual[0] = jnp.zeros(residual.shape[1:], jnp.float32)

    @pl.when(row == row_count - 1)
    def _():
        residual[2] = jnp.zeros(residual.shape[1:], jnp.float32)

    def ramped(n):
        flat = residual[n].reshape(-1, TILE)
        return jnp.dot(
            flat,
            ramp_ref[n],
            precision=lax.Precision.HIGHEST,
            preferred_element_type=jnp.float32,
        )

    result = ramped(1)

    @pl.when(row > 0)
    def _():
        after.wait_recv()

    @pl.when(row < row_count - 1)
    def _():
        before.wait_recv()

    result = result + ramped(0) + ramped(2)
    filtered[row] = result.astype(jnp.bfloat16).reshape(filtered.shape[1:])

    gathers = []
    for k in range(1, row_count):
        peer = lax.rem(row + k, row_count)
        gathers.append(send(filtered.at[row], filtered.at[row], filter_sems, k, peer, col))
        gathers[-1].start()
    for k in range(1, row_count):
        source = lax.rem(row + row_count - k, row_count)
        send(
            filtered.at[source], filtered.at[source], filter_sems, k, source, col
        ).wait_recv()

    def window(peer):
        target = target_ref[peer]
        value = jnp.zeros(target.shape, jnp.float32)
        for block in range(row_count):
            piece = filtered[block].astype(jnp.float32)[:, None]
            value = jnp.where(target == block, piece, value)
        return value.astype(jnp.bfloat16)

    moves = []
    for k in range(1, col_count):
        peer = lax.rem(col + k, col_count)
        windows[k] = window(peer)
        moves.append(send(windows.at[k], landed.at[col], window_sems, k, row, peer))
        moves[-1].start()
    landed[col] = window(col)
    for move in moves:
        move.wait_recv()
    out_ref[...] = landed[...]

    for copy in copies + sums + gathers + moves:
        copy.wait_send()

    @pl.when(row > 0)
    def _():
        before.wait_send()

    @pl.when(row < row_count - 1)
    def _():
        after.wait_send()


def exchange(partial_value, target, measured, ray_weight):
    row_count = lax.axis_size("row")
    col_count = lax.axis_size("col")
    angles, across, slices, unused = partial_value.shape
    here = angles // col_count
    in_bins = jnp.arange(TILE, dtype=jnp.int32)
    ramps = jnp.stack(
        [ramp(in_bins[None, :] - in_bins[:, None] - n * TILE) for n in (-1, 0, 1)]
    )
    shape = (col_count, here, across, slices, TILE)
    dma = pltpu.SemaphoreType.DMA
    vmem = pl.BlockSpec(memory_space=pltpu.VMEM)
    target = jnp.broadcast_to(target[:, :, :, None, :], shape)
    block = (here, slices, TILE)
    result = pl.pallas_call(
        exchange_kernel,
        out_shape=jax.ShapeDtypeStruct(shape, jnp.bfloat16),
        in_specs=[vmem] * 5,
        out_specs=vmem,
        scratch_shapes=[
            pltpu.VMEM(shape, jnp.bfloat16),
            pltpu.VMEM((row_count,) + block, jnp.bfloat16),
            pltpu.VMEM((row_count,) + block, jnp.bfloat16),
            pltpu.VMEM((3,) + block, jnp.float32),
            pltpu.VMEM((row_count,) + block, jnp.bfloat16),
            pltpu.VMEM(shape, jnp.bfloat16),
            pltpu.VMEM(shape, jnp.bfloat16),
            dma((2, col_count)),
            dma((2, row_count)),
            dma((2, 2)),
            dma((2, row_count)),
            dma((2, col_count)),
        ],
        compiler_params=pltpu.CompilerParams(collective_id=0, has_side_effects=True),
        name="exchange",
    )(
        partial_value.reshape(shape),
        target,
        measured.reshape(block),
        ray_weight.reshape(here, 1, TILE),
        ramps,
    )
    return result.reshape(partial_value.shape)


def edges_kernel(row_edge, col_edge, row_out, col_out, row_halo, col_halo, sems):
    row_count = lax.axis_size("row")
    col_count = lax.axis_size("col")
    row = lax.axis_index("row")
    col = lax.axis_index("col")
    groups = col_edge.shape[1]
    row_halo[...] = jnp.zeros(row_halo.shape, jnp.float32)
    col_halo[...] = jnp.zeros(col_halo.shape, jnp.float32)
    inner = pl.ds(1, groups)
    routes = (
        (-1, 0, row_edge.at[0], row_halo.at[1]),
        (1, 0, row_edge.at[1], row_halo.at[0]),
        (0, -1, col_edge.at[0], col_halo.at[1, inner]),
        (0, 1, col_edge.at[1], col_halo.at[0, inner]),
        (-1, -1, col_edge.at[0, 0], col_halo.at[1, groups + 1]),
        (-1, 1, col_edge.at[1, 0], col_halo.at[0, groups + 1]),
        (1, -1, col_edge.at[0, groups - 1], col_halo.at[1, 0]),
        (1, 1, col_edge.at[1, groups - 1], col_halo.at[0, 0]),
    )

    def exists(down, right):
        to_row, to_col = row + down, col + right
        return (to_row >= 0) & (to_row < row_count) & (to_col >= 0) & (to_col < col_count)

    barrier = pltpu.get_barrier_semaphore()
    for down, right, src, dst in routes:

        @pl.when(exists(down, right))
        def _(down=down, right=right):
            pl.semaphore_signal(
                barrier, inc=1, device_id=(row + down, col + right), device_id_type=MESH
            )

    rows_near = jnp.where(row > 0, 1, 0) + jnp.where(row < row_count - 1, 1, 0)
    cols_near = jnp.where(col > 0, 1, 0) + jnp.where(col < col_count - 1, 1, 0)
    pl.semaphore_wait(barrier, (rows_near + 1) * (cols_near + 1) - 1)

    copies = []
    for k, (down, right, src, dst) in enumerate(routes):
        copy = pltpu.make_async_remote_copy(
            src_ref=src,
            dst_ref=dst,
            send_sem=sems.at[0, k],
            recv_sem=sems.at[1, k],
            device_id=(row + down, col + right),
            device_id_type=MESH,
        )
        copies.append((down, right, copy))
        pl.when(exists(down, right))(copy.start)
    for down, right, copy in copies:
        pl.when(exists(-down, -right))(copy.wait_recv)
    row_out[...] = row_halo[...]
    col_out[...] = col_halo[...]
    for down, right, copy in copies:
        pl.when(exists(down, right))(copy.wait_send)


def exchange_edges(row_edge, col_edge):
    vmem = pl.BlockSpec(memory_space=pltpu.VMEM)
    wide = (2, col_edge.shape[1] + 2) + col_edge.shape[2:]
    return pl.pallas_call(
        edges_kernel,
        out_shape=[
            jax.ShapeDtypeStruct(row_edge.shape, jnp.float32),
            jax.ShapeDtypeStruct(wide, jnp.float32),
        ],
        in_specs=[vmem] * 2,
        out_specs=[vmem] * 2,
        scratch_shapes=[
            pltpu.VMEM(row_edge.shape, jnp.float32),
            pltpu.VMEM(wide, jnp.float32),
            pltpu.SemaphoreType.DMA((2, 8)),
        ],
        compiler_params=pltpu.CompilerParams(collective_id=1, has_side_effects=True),
        name="exchange_edges",
    )(row_edge, col_edge)


ROWS = 16


def smooth_kernel(near_ref, x_ref, row_halo, col_halo, out_ref, y_ref):
    height, slices, width = x_ref.shape
    full = width + TILE
    lanes = lax.broadcasted_iota(jnp.int32, (slices, TILE), 1)
    lanes8 = lax.broadcasted_iota(jnp.int32, (8, TILE), 1)
    above, below = near_ref[0] > 0, near_ref[1] > 0
    spot = lax.broadcasted_iota(jnp.int32, (slices, full), 1)
    kept = (
        (spot < width)
        | ((spot < width + TV_STEPS) & (near_ref[3] > 0))
        | ((spot >= full - TV_STEPS) & (near_ref[2] > 0))
    )
    y_ref[0:TV_STEPS, :, 0:width] = row_halo[0]
    y_ref[TV_STEPS + height : 2 * TV_STEPS + height, :, 0:width] = row_halo[1]

    def fill(w, carry):
        place = w + PACK - TV_STEPS
        group = place // PACK
        offset = lax.rem(place, PACK) * TV_STEPS
        for g in range(slices // 8):
            span = slice(g * 8, g * 8 + 8)
            left = lookup(
                col_halo[0, group, span], (lanes8 + (TV_STEPS + offset)) & (TILE - 1)
            )
            right = lookup(col_halo[1, group, span], (lanes8 + offset) & (TILE - 1))
            y_ref[w, span, width:] = jnp.where(
                lanes8 >= TILE - TV_STEPS, left, jnp.where(lanes8 < TV_STEPS, right, 0.0)
            )
        return carry

    lax.fori_loop(0, height + 2 * TV_STEPS, fill, jnp.int32(0), unroll=8)
    spare = y_ref.shape[0] - height - 2 * TV_STEPS
    y_ref[height + 2 * TV_STEPS :] = jnp.zeros((spare, slices, full), jnp.float32)

    def copy(u, carry):
        y_ref[u + TV_STEPS, :, 0:width] = x_ref[u]
        return carry

    lax.fori_loop(0, height, copy, jnp.int32(0), unroll=8)

    def flows(here, after):
        down = after - here
        across = pltpu.roll(here, full - 1, 1) - here
        scale = lax.rsqrt(smoothing * smoothing + down * down + across * across)
        return down * scale, across * scale

    for step in range(TV_STEPS):
        flow = flows(y_ref[step], y_ref[step + 1])[0]

        def some_rows(block, above_flow, step=step):
            w = step + 1 + block * ROWS
            olds = [y_ref[w + k] for k in range(ROWS + 1)]
            news = []
            for k in range(ROWS):
                flow_down, flow_right = flows(olds[k], olds[k + 1])
                gradient = above_flow - flow_down + pltpu.roll(flow_right, 1, 1) - flow_right
                news.append(olds[k] - descent_step * gradient)
                above_flow = flow_down
            for k, value in enumerate(news):
                if step == TV_STEPS - 1:
                    out_ref[w + k - TV_STEPS] = value[:, 0:width]
                else:
                    row = w + k
                    inside = ((row >= TV_STEPS) | above) & ((row < height + TV_STEPS) | below)
                    y_ref[row] = jnp.where(kept, value, 0.0) * jnp.where(inside, 1.0, 0.0)
            return above_flow

        rows = height + 2 * (TV_STEPS - 1 - step)
        lax.fori_loop(0, pl.cdiv(rows, ROWS), some_rows, flow)


def smooth(x, row_halo, col_halo, near):
    height, slices, width = x.shape
    vmem = pl.BlockSpec(memory_space=pltpu.VMEM)
    return pl.pallas_call(
        smooth_kernel,
        out_shape=jax.ShapeDtypeStruct(x.shape, jnp.float32),
        in_specs=[pl.BlockSpec(memory_space=pltpu.SMEM)] + [vmem] * 3,
        out_specs=vmem,
        scratch_shapes=[pltpu.VMEM((height + 2 * TV_STEPS + ROWS, slices, width + TILE), jnp.float32)],
        compiler_params=pltpu.CompilerParams(vmem_limit_bytes=48 << 20),
        name="smooth",
    )(near, x, row_halo, col_halo)


def local(current_image, measured, ray_weight, angle_ids, shadow_start):
    row_index = lax.axis_index("row")
    col_index = lax.axis_index("col")
    row_count = lax.axis_size("row")
    col_count = lax.axis_size("col")
    slices = current_image.shape[0]
    local_width = current_image.shape[2]
    across = local_width // TILE
    angles_here = ANGLES // col_count
    table = angle_table(angle_ids)
    rows = current_image.transpose(1, 0, 2)
    rounded = current_image.astype(jnp.bfloat16)
    columns = rounded.reshape(slices, TILE, across, TILE).transpose(3, 0, 2, 1)
    lines = jnp.stack([rounded.transpose(1, 0, 2), columns.reshape(TILE, slices, local_width)])
    row_starts = shadow_start[row_index]
    own_starts = lax.dynamic_slice_in_dim(row_starts, col_index * across, across, 0)

    shift = own_starts.T % TILE
    partial_value = project(lines, table, shift)
    wanted = lax.dynamic_slice_in_dim(row_starts, col_index * angles_here, angles_here, 1)
    lane = jnp.arange(TILE, dtype=jnp.int32)
    target = wanted[:, :, None] // TILE + (lane < wanted[:, :, None] % TILE)
    target = target.reshape(col_count, across, angles_here, TILE).transpose(0, 2, 1, 3)
    shadows = exchange(partial_value, target.astype(jnp.int32), measured, ray_weight)
    current, row_edge, col_edge = back_project(shadows, rows, table, shift)
    row_halo, col_halo = exchange_edges(row_edge, col_edge)
    near = jnp.stack(
        [row_index > 0, row_index < row_count - 1, col_index > 0, col_index < col_count - 1]
    ).astype(jnp.int32)
    current = smooth(current, row_halo, col_halo, near).transpose(1, 0, 2)
    return current


def solution(mesh):
    return jax.shard_map(
        local,
        mesh=mesh,
        in_specs=(
            P(None, "row", "col"),
            P("col", "row", None, None),
            P("col", "row", None),
            P(),
            P(),
        ),
        out_specs=P(None, "row", "col"),
        check_vma=False,
    )
```

```python
import math

import jax
import jax.numpy as jnp
from jax import lax
from jax.experimental import pallas as pl
from jax.experimental.pallas import tpu as pltpu
from jax.sharding import PartitionSpec as P

TILE = 128
ANGLES = 16
ALL_ANGLES = 256
TV_STEPS = 4
PACK = TILE // TV_STEPS


inverse_root = 0.7071067811865476
proj_scale = 0.03125
relaxation = 8.0
smoothing = 0.25
descent_step = 0.05


def angle_table(angle_ids):
    radians = angle_ids.astype(jnp.float32) * (math.pi / ALL_ANGLES)
    row_step = jnp.cos(radians) * inverse_root
    col_step = jnp.sin(radians) * inverse_root
    steep = jnp.where(jnp.abs(col_step) >= jnp.abs(row_step), 0, 1).astype(jnp.int32)
    return row_step, col_step, steep


def lookup(table, index):
    return jnp.take_along_axis(table, index, axis=1, mode="promise_in_bounds")


def pieces(slices, across):
    return [(t, g) for t in range(across) for g in range(slices // 8)]


LINES = 8


def forward_kernel(
    slow_ref, fast_ref, steep_ref, shift_ref, x_ref, prefix_ref, out_ref, once_ref, twice_ref
):
    slices = x_ref.shape[2]
    across = x_ref.shape[3] // TILE
    groups = slices // 8
    count = across * groups
    centre = (TILE - 1) / 2.0
    whole_lanes = lax.broadcasted_iota(jnp.int32, (8, TILE), 1)
    lanes = whole_lanes.astype(jnp.float32)
    following = (whole_lanes + 1) & (TILE - 1)
    preceding = (whole_lanes - 1) & (TILE - 1)

    def fill(block, carry):
        at = pl.multiple_of(block * LINES, LINES)
        for way in range(2):
            for tile in range(across):
                flat = x_ref[way, pl.ds(at, LINES), :, tile * TILE : (tile + 1) * TILE]
                both = jnp.dot(
                    flat.reshape(LINES * slices, TILE),
                    prefix_ref[...],
                    preferred_element_type=jnp.float32,
                ).reshape(LINES, groups, 8, 2 * TILE)
                span = slice(tile * groups, (tile + 1) * groups)
                once_ref[way, pl.ds(at, LINES), span] = both[..., :TILE]
                twice_ref[way, pl.ds(at, LINES), span] = both[..., TILE:]
        return carry

    lax.fori_loop(0, TILE // LINES, fill, jnp.int32(0))
    zero = jnp.zeros((8, TILE), jnp.float32)

    def add_line(line, sums):
        return tuple(sums[n] + once_ref[0, line, n] for n in range(count))

    totals = lax.fori_loop(0, TILE, add_line, (zero,) * count)
    totals = [lookup(t, jnp.full((8, TILE), TILE - 1, jnp.int32)) for t in totals]

    def one_angle(a, carry):
        slow = slow_ref[a]
        fast = jnp.full((8, TILE), fast_ref[a], jnp.float32)
        steep = steep_ref[a]
        inverse = 1.0 / fast
        base = (lanes + (0.5 - TILE / 2.0)) * inverse + centre
        tilt = slow * inverse

        def some_lines(block, sums):
            here = [zero] * count
            for k in range(LINES):
                line = block * LINES + k
                q = jnp.maximum(base - (line.astype(jnp.float32) - centre) * tilt, 0.0)
                whole = jnp.minimum(jnp.floor(q), TILE - 1.0)
                part = q - whole
                index = whole.astype(jnp.int32)
                first = [lookup(once_ref[steep, line, n], index) for n in range(count)]
                second = [lookup(twice_ref[steep, line, n], index) for n in range(count)]
                for n in range(count):
                    here[n] = here[n] + (second[n] + part * first[n])
            return tuple(
                sums[n] + (lookup(here[n], following) - here[n]) for n in range(count)
            )

        sums = lax.fori_loop(0, TILE // LINES, some_lines, (zero,) * count, unroll=8)
        sent = []
        for n in range(count):
            tile = n // groups
            beyond = totals[n] * inverse
            last = jnp.where(fast > 0, beyond, 0.0)
            before = jnp.where(fast > 0, 0.0, beyond)
            steps = jnp.where(whole_lanes == TILE - 1, last, sums[n])
            earlier = jnp.where(whole_lanes == 0, before, lookup(steps, preceding))
            shadow = (steps - earlier) * (jnp.abs(fast) * proj_scale)
            turned = lookup(shadow, (whole_lanes - shift_ref[a, tile]) & (TILE - 1))
            sent.append(turned)
        for tile in range(across):
            both = jnp.concatenate(sent[tile * groups : (tile + 1) * groups], axis=0)
            out_ref[a, tile] = both.astype(out_ref.dtype)
        return carry

    lax.fori_loop(0, slow_ref.shape[0], one_angle, jnp.int32(0))


def project(lines, table, shift):
    row_step, col_step, steep = table
    slow = jnp.where(steep == 0, row_step, col_step)
    fast = jnp.where(steep == 0, col_step, row_step)
    slices = lines.shape[2]
    across = lines.shape[3] // TILE
    spot = jnp.arange(TILE, dtype=jnp.int32)
    gap = spot[None, :] - spot[:, None]
    prefix = jnp.concatenate([gap >= 0, jnp.maximum(gap, 0)], axis=1).astype(jnp.bfloat16)
    smem = pl.BlockSpec(memory_space=pltpu.SMEM)
    vmem = pl.BlockSpec(memory_space=pltpu.VMEM)
    held = pltpu.VMEM((2, TILE, across * slices // 8, 8, TILE), jnp.float32)
    return pl.pallas_call(
        forward_kernel,
        out_shape=jax.ShapeDtypeStruct((ANGLES, across, slices, TILE), jnp.bfloat16),
        in_specs=[smem, smem, smem, smem, vmem, vmem],
        out_specs=vmem,
        scratch_shapes=[held, held],
        compiler_params=pltpu.CompilerParams(vmem_limit_bytes=48 << 20),
        name="project",
    )(slow, fast, steep, shift, lines, prefix)


def backward_kernel(
    row_ref,
    col_ref,
    shift_ref,
    shadow_ref,
    x_ref,
    out_ref,
    row_edge_ref,
    col_edge_ref,
    value_ref,
    step_ref,
    base_ref,
):
    slices = x_ref.shape[1]
    across = x_ref.shape[2] // TILE
    angles = shadow_ref.shape[0]
    parts = pieces(slices, across)
    centre = (TILE - 1) / 2.0
    whole_lanes = lax.broadcasted_iota(jnp.int32, (8, TILE), 1)
    lanes = whole_lanes.astype(jnp.float32) - centre
    scale = relaxation * proj_scale
    for a in range(angles):
        base_ref[a] = TILE / 2.0 - 0.5 + lanes * col_ref[a]
        for n, (tile, group) in enumerate(parts):
            value = shadow_ref[a, tile, group * 8 : group * 8 + 8, :].astype(jnp.float32) * scale
            value = lookup(value, (whole_lanes + shift_ref[a, tile]) & (TILE - 1))
            value_ref[a, n] = value
            step_ref[a, n] = jnp.roll(value, -1, axis=1) - value

    def one_row(u, carry):
        place = u.astype(jnp.float32) - centre
        sums = [
            x_ref[u, g * 8 : g * 8 + 8, t * TILE : (t + 1) * TILE].astype(jnp.float32)
            for t, g in parts
        ]
        for a in range(angles):
            z = base_ref[a] + place * row_ref[a]
            z = jnp.minimum(jnp.maximum(z, 0.0), TILE - 1.00001)
            whole = jnp.floor(z)
            part = z - whole
            index = whole.astype(jnp.int32)
            for n in range(len(parts)):
                sums[n] = sums[n] + (
                    lookup(value_ref[a, n], index) + part * lookup(step_ref[a, n], index)
                )
        for n, (t, g) in enumerate(parts):
            out_ref[u, g * 8 : g * 8 + 8, t * TILE : (t + 1) * TILE] = sums[n]
        return carry

    lax.fori_loop(0, TILE, one_row, jnp.int32(0), unroll=2)

    def pack(block, carry):
        for side, tile, start in ((0, 0, 0), (1, across - 1, TILE - TV_STEPS)):
            for g in range(slices // 8):
                span = slice(g * 8, g * 8 + 8)
                packed = jnp.zeros((8, TILE), jnp.float32)
                for r in range(PACK):
                    offset = r * TV_STEPS
                    inside = (whole_lanes >= offset) & (whole_lanes < offset + TV_STEPS)
                    row = out_ref[block * PACK + r, span, tile * TILE : (tile + 1) * TILE]
                    moved = lookup(row, (whole_lanes + (start - offset)) & (TILE - 1))
                    packed = jnp.where(inside, moved, packed)
                col_edge_ref[side, block, span] = packed
        return carry

    lax.fori_loop(0, TILE // PACK, pack, jnp.int32(0))
    row_edge_ref[0] = out_ref[0:TV_STEPS]
    row_edge_ref[1] = out_ref[TILE - TV_STEPS : TILE]


def back_project(shadows, rows, table, shift):
    row_step, col_step, steep = table
    angles, across, slices, unused = shadows.shape
    smem = pl.BlockSpec(memory_space=pltpu.SMEM)
    vmem = pl.BlockSpec(memory_space=pltpu.VMEM)
    parts = across * slices // 8
    return pl.pallas_call(
        backward_kernel,
        out_shape=[
            jax.ShapeDtypeStruct(rows.shape, jnp.float32),
            jax.ShapeDtypeStruct((2, TV_STEPS) + rows.shape[1:], jnp.float32),
            jax.ShapeDtypeStruct((2, TILE // PACK, slices, TILE), jnp.float32),
        ],
        in_specs=[smem, smem, smem, vmem, vmem],
        out_specs=[vmem] * 3,
        scratch_shapes=[
            pltpu.VMEM((angles, parts, 8, TILE), jnp.float32),
            pltpu.VMEM((angles, parts, 8, TILE), jnp.float32),
            pltpu.VMEM((angles, 8, TILE), jnp.float32),
        ],
        name="back_project",
    )(row_step, col_step, shift, shadows, rows)


def ramp(offset):
    is_odd = offset % 2 != 0
    nonzero = jnp.where(offset == 0, 1, offset).astype(jnp.float32)
    values = jnp.where(is_odd, -1.0 / (math.pi * math.pi * nonzero * nonzero), 0.0)
    values = jnp.where(offset == 0, 0.25, values)
    return jnp.where(jnp.abs(offset) < TILE, values, 0.0)


MESH = pl.DeviceIdType.MESH


def exchange_kernel(
    partial_ref,
    target_ref,
    measured_ref,
    weight_ref,
    ramp_ref,
    out_ref,
    tiles,
    outgoing,
    incoming,
    residual,
    filtered,
    windows,
    landed,
    tile_sems,
    sum_sems,
    edge_sems,
    filter_sems,
    window_sems,
):
    row_count = lax.axis_size("row")
    col_count = lax.axis_size("col")
    row = lax.axis_index("row")
    col = lax.axis_index("col")
    here = measured_ref.shape[0]

    def send(src, dst, sems, k, to_row, to_col):
        return pltpu.make_async_remote_copy(
            src_ref=src,
            dst_ref=dst,
            send_sem=sems.at[0, k],
            recv_sem=sems.at[1, k],
            device_id=(to_row, to_col),
            device_id_type=MESH,
        )

    barrier = pltpu.get_barrier_semaphore()
    for k in range(1, col_count):
        pl.semaphore_signal(
            barrier, inc=1, device_id=(row, lax.rem(col + k, col_count)), device_id_type=MESH
        )
    for k in range(1, row_count):
        pl.semaphore_signal(
            barrier, inc=1, device_id=(lax.rem(row + k, row_count), col), device_id_type=MESH
        )
    pl.semaphore_wait(barrier, col_count + row_count - 2)

    copies = []
    for k in range(1, col_count):
        peer = lax.rem(col + k, col_count)
        copies.append(
            send(partial_ref.at[peer], tiles.at[col], tile_sems, k, row, peer)
        )
        copies[-1].start()
    tiles[col] = partial_ref[col]
    for k in range(1, col_count):
        copies[k - 1].wait_recv()

    def summed(block):
        chosen = jnp.where(target_ref[...] == block, tiles[...].astype(jnp.float32), 0.0)
        return jnp.sum(jnp.sum(chosen, axis=2), axis=0)

    sums = []
    for k in range(1, row_count):
        peer = lax.rem(row + k, row_count)
        outgoing[k] = summed(peer).astype(outgoing.dtype)
        sums.append(send(outgoing.at[k], incoming.at[k], sum_sems, k, peer, col))
        sums[-1].start()
    total = summed(row)
    for k in range(1, row_count):
        sums[k - 1].wait_recv()
        total = total + incoming[k].astype(jnp.float32)
    residual[1] = weight_ref[...] * (measured_ref[...] - total)

    before = send(residual.at[1], residual.at[2], edge_sems, 0, row - 1, col)
    after = send(residual.at[1], residual.at[0], edge_sems, 1, row + 1, col)

    @pl.when(row > 0)
    def _():
        before.start()

    @pl.when(row < row_count - 1)
    def _():
        after.start()

    @pl.when(row == 0)
    def _():
        residual[0] = jnp.zeros(residual.shape[1:], jnp.float32)

    @pl.when(row == row_count - 1)
    def _():
        residual[2] = jnp.zeros(residual.shape[1:], jnp.float32)

    def ramped(n):
        flat = residual[n].reshape(-1, TILE)
        return jnp.dot(
            flat,
            ramp_ref[n],
            precision=lax.Precision.HIGHEST,
            preferred_element_type=jnp.float32,
        )

    result = ramped(1)

    @pl.when(row > 0)
    def _():
        after.wait_recv()

    @pl.when(row < row_count - 1)
    def _():
        before.wait_recv()

    result = result + ramped(0) + ramped(2)
    filtered[row] = result.astype(jnp.bfloat16).reshape(filtered.shape[1:])

    gathers = []
    for k in range(1, row_count):
        peer = lax.rem(row + k, row_count)
        gathers.append(send(filtered.at[row], filtered.at[row], filter_sems, k, peer, col))
        gathers[-1].start()
    for k in range(1, row_count):
        source = lax.rem(row + row_count - k, row_count)
        send(
            filtered.at[source], filtered.at[source], filter_sems, k, source, col
        ).wait_recv()

    def window(peer):
        target = target_ref[peer]
        value = jnp.zeros(target.shape, jnp.float32)
        for block in range(row_count):
            piece = filtered[block].astype(jnp.float32)[:, None]
            value = jnp.where(target == block, piece, value)
        return value.astype(jnp.bfloat16)

    moves = []
    for k in range(1, col_count):
        peer = lax.rem(col + k, col_count)
        windows[k] = window(peer)
        moves.append(send(windows.at[k], landed.at[col], window_sems, k, row, peer))
        moves[-1].start()
    landed[col] = window(col)
    for move in moves:
        move.wait_recv()
    out_ref[...] = landed[...]

    for copy in copies + sums + gathers + moves:
        copy.wait_send()

    @pl.when(row > 0)
    def _():
        before.wait_send()

    @pl.when(row < row_count - 1)
    def _():
        after.wait_send()


def exchange(partial_value, target, measured, ray_weight):
    row_count = lax.axis_size("row")
    col_count = lax.axis_size("col")
    angles, across, slices, unused = partial_value.shape
    here = angles // col_count
    in_bins = jnp.arange(TILE, dtype=jnp.int32)
    ramps = jnp.stack(
        [ramp(in_bins[None, :] - in_bins[:, None] - n * TILE) for n in (-1, 0, 1)]
    )
    shape = (col_count, here, across, slices, TILE)
    dma = pltpu.SemaphoreType.DMA
    vmem = pl.BlockSpec(memory_space=pltpu.VMEM)
    target = jnp.broadcast_to(target[:, :, :, None, :], shape)
    block = (here, slices, TILE)
    result = pl.pallas_call(
        exchange_kernel,
        out_shape=jax.ShapeDtypeStruct(shape, jnp.bfloat16),
        in_specs=[vmem] * 5,
        out_specs=vmem,
        scratch_shapes=[
            pltpu.VMEM(shape, jnp.bfloat16),
            pltpu.VMEM((row_count,) + block, jnp.bfloat16),
            pltpu.VMEM((row_count,) + block, jnp.bfloat16),
            pltpu.VMEM((3,) + block, jnp.float32),
            pltpu.VMEM((row_count,) + block, jnp.bfloat16),
            pltpu.VMEM(shape, jnp.bfloat16),
            pltpu.VMEM(shape, jnp.bfloat16),
            dma((2, col_count)),
            dma((2, row_count)),
            dma((2, 2)),
            dma((2, row_count)),
            dma((2, col_count)),
        ],
        compiler_params=pltpu.CompilerParams(collective_id=0, has_side_effects=True),
        name="exchange",
    )(
        partial_value.reshape(shape),
        target,
        measured.reshape(block),
        ray_weight.reshape(here, 1, TILE),
        ramps,
    )
    return result.reshape(partial_value.shape)


def edges_kernel(row_edge, col_edge, row_out, col_out, row_halo, col_halo, sems):
    row_count = lax.axis_size("row")
    col_count = lax.axis_size("col")
    row = lax.axis_index("row")
    col = lax.axis_index("col")
    groups = col_edge.shape[1]
    row_halo[...] = jnp.zeros(row_halo.shape, jnp.float32)
    col_halo[...] = jnp.zeros(col_halo.shape, jnp.float32)
    inner = pl.ds(1, groups)
    routes = (
        (-1, 0, row_edge.at[0], row_halo.at[1]),
        (1, 0, row_edge.at[1], row_halo.at[0]),
        (0, -1, col_edge.at[0], col_halo.at[1, inner]),
        (0, 1, col_edge.at[1], col_halo.at[0, inner]),
        (-1, -1, col_edge.at[0, 0], col_halo.at[1, groups + 1]),
        (-1, 1, col_edge.at[1, 0], col_halo.at[0, groups + 1]),
        (1, -1, col_edge.at[0, groups - 1], col_halo.at[1, 0]),
        (1, 1, col_edge.at[1, groups - 1], col_halo.at[0, 0]),
    )

    def exists(down, right):
        to_row, to_col = row + down, col + right
        return (to_row >= 0) & (to_row < row_count) & (to_col >= 0) & (to_col < col_count)

    barrier = pltpu.get_barrier_semaphore()
    for down, right, src, dst in routes:

        @pl.when(exists(down, right))
        def _(down=down, right=right):
            pl.semaphore_signal(
                barrier, inc=1, device_id=(row + down, col + right), device_id_type=MESH
            )

    rows_near = jnp.where(row > 0, 1, 0) + jnp.where(row < row_count - 1, 1, 0)
    cols_near = jnp.where(col > 0, 1, 0) + jnp.where(col < col_count - 1, 1, 0)
    pl.semaphore_wait(barrier, (rows_near + 1) * (cols_near + 1) - 1)

    copies = []
    for k, (down, right, src, dst) in enumerate(routes):
        copy = pltpu.make_async_remote_copy(
            src_ref=src,
            dst_ref=dst,
            send_sem=sems.at[0, k],
            recv_sem=sems.at[1, k],
            device_id=(row + down, col + right),
            device_id_type=MESH,
        )
        copies.append((down, right, copy))
        pl.when(exists(down, right))(copy.start)
    for down, right, copy in copies:
        pl.when(exists(-down, -right))(copy.wait_recv)
    row_out[...] = row_halo[...]
    col_out[...] = col_halo[...]
    for down, right, copy in copies:
        pl.when(exists(down, right))(copy.wait_send)


def exchange_edges(row_edge, col_edge):
    vmem = pl.BlockSpec(memory_space=pltpu.VMEM)
    wide = (2, col_edge.shape[1] + 2) + col_edge.shape[2:]
    return pl.pallas_call(
        edges_kernel,
        out_shape=[
            jax.ShapeDtypeStruct(row_edge.shape, jnp.float32),
            jax.ShapeDtypeStruct(wide, jnp.float32),
        ],
        in_specs=[vmem] * 2,
        out_specs=[vmem] * 2,
        scratch_shapes=[
            pltpu.VMEM(row_edge.shape, jnp.float32),
            pltpu.VMEM(wide, jnp.float32),
            pltpu.SemaphoreType.DMA((2, 8)),
        ],
        compiler_params=pltpu.CompilerParams(collective_id=1, has_side_effects=True),
        name="exchange_edges",
    )(row_edge, col_edge)


ROWS = 8


def smooth_kernel(near_ref, x_ref, row_halo, col_halo, out_ref, y_ref):
    height, slices, width = x_ref.shape
    full = width + TILE
    lanes = lax.broadcasted_iota(jnp.int32, (slices, TILE), 1)
    lanes8 = lax.broadcasted_iota(jnp.int32, (8, TILE), 1)
    above, below = near_ref[0] > 0, near_ref[1] > 0
    spot = lax.broadcasted_iota(jnp.int32, (slices, full), 1)
    kept = (
        (spot < width)
        | ((spot < width + TV_STEPS) & (near_ref[3] > 0))
        | ((spot >= full - TV_STEPS) & (near_ref[2] > 0))
    )
    y_ref[0:TV_STEPS, :, 0:width] = row_halo[0]
    y_ref[TV_STEPS + height : 2 * TV_STEPS + height, :, 0:width] = row_halo[1]

    def fill(w, carry):
        place = w + PACK - TV_STEPS
        group = place // PACK
        offset = lax.rem(place, PACK) * TV_STEPS
        for g in range(slices // 8):
            span = slice(g * 8, g * 8 + 8)
            left = lookup(
                col_halo[0, group, span], (lanes8 + (TV_STEPS + offset)) & (TILE - 1)
            )
            right = lookup(col_halo[1, group, span], (lanes8 + offset) & (TILE - 1))
            y_ref[w, span, width:] = jnp.where(
                lanes8 >= TILE - TV_STEPS, left, jnp.where(lanes8 < TV_STEPS, right, 0.0)
            )
        return carry

    lax.fori_loop(0, height + 2 * TV_STEPS, fill, jnp.int32(0), unroll=8)
    spare = y_ref.shape[0] - height - 2 * TV_STEPS
    y_ref[height + 2 * TV_STEPS :] = jnp.zeros((spare, slices, full), jnp.float32)

    def copy(u, carry):
        y_ref[u + TV_STEPS, :, 0:width] = x_ref[u]
        return carry

    lax.fori_loop(0, height, copy, jnp.int32(0), unroll=8)

    def flows(here, after):
        down = after - here
        across = pltpu.roll(here, full - 1, 1) - here
        scale = lax.rsqrt(smoothing * smoothing + down * down + across * across)
        return down * scale, across * scale

    for step in range(TV_STEPS):
        flow = flows(y_ref[step], y_ref[step + 1])[0]

        def some_rows(block, above_flow, step=step):
            w = step + 1 + block * ROWS
            olds = [y_ref[w + k] for k in range(ROWS + 1)]
            news = []
            for k in range(ROWS):
                flow_down, flow_right = flows(olds[k], olds[k + 1])
                gradient = above_flow - flow_down + pltpu.roll(flow_right, 1, 1) - flow_right
                news.append(olds[k] - descent_step * gradient)
                above_flow = flow_down
            for k, value in enumerate(news):
                if step == TV_STEPS - 1:
                    out_ref[w + k - TV_STEPS] = value[:, 0:width]
                else:
                    row = w + k
                    inside = ((row >= TV_STEPS) | above) & ((row < height + TV_STEPS) | below)
                    y_ref[row] = jnp.where(kept, value, 0.0) * jnp.where(inside, 1.0, 0.0)
            return above_flow

        rows = height + 2 * (TV_STEPS - 1 - step)
        lax.fori_loop(0, pl.cdiv(rows, ROWS), some_rows, flow)


def smooth(x, row_halo, col_halo, near):
    height, slices, width = x.shape
    vmem = pl.BlockSpec(memory_space=pltpu.VMEM)
    return pl.pallas_call(
        smooth_kernel,
        out_shape=jax.ShapeDtypeStruct(x.shape, jnp.float32),
        in_specs=[pl.BlockSpec(memory_space=pltpu.SMEM)] + [vmem] * 3,
        out_specs=vmem,
        scratch_shapes=[pltpu.VMEM((height + 2 * TV_STEPS + ROWS, slices, width + TILE), jnp.float32)],
        compiler_params=pltpu.CompilerParams(vmem_limit_bytes=48 << 20),
        name="smooth",
    )(near, x, row_halo, col_halo)


def local(current_image, measured, ray_weight, angle_ids, shadow_start):
    row_index = lax.axis_index("row")
    col_index = lax.axis_index("col")
    row_count = lax.axis_size("row")
    col_count = lax.axis_size("col")
    slices = current_image.shape[0]
    local_width = current_image.shape[2]
    across = local_width // TILE
    angles_here = ANGLES // col_count
    table = angle_table(angle_ids)
    rows = current_image.transpose(1, 0, 2)
    rounded = current_image.astype(jnp.bfloat16)
    columns = rounded.reshape(slices, TILE, across, TILE).transpose(3, 0, 2, 1)
    lines = jnp.stack([rounded.transpose(1, 0, 2), columns.reshape(TILE, slices, local_width)])
    row_starts = shadow_start[row_index]
    own_starts = lax.dynamic_slice_in_dim(row_starts, col_index * across, across, 0)

    shift = own_starts.T % TILE
    partial_value = project(lines, table, shift)
    wanted = lax.dynamic_slice_in_dim(row_starts, col_index * angles_here, angles_here, 1)
    lane = jnp.arange(TILE, dtype=jnp.int32)
    target = wanted[:, :, None] // TILE + (lane < wanted[:, :, None] % TILE)
    target = target.reshape(col_count, across, angles_here, TILE).transpose(0, 2, 1, 3)
    shadows = exchange(partial_value, target.astype(jnp.int32), measured, ray_weight)
    current, row_edge, col_edge = back_project(shadows, rows, table, shift)
    row_halo, col_halo = exchange_edges(row_edge, col_edge)
    near = jnp.stack(
        [row_index > 0, row_index < row_count - 1, col_index > 0, col_index < col_count - 1]
    ).astype(jnp.int32)
    current = smooth(current, row_halo, col_halo, near).transpose(1, 0, 2)
    return current


def solution(mesh):
    return jax.shard_map(
        local,
        mesh=mesh,
        in_specs=(
            P(None, "row", "col"),
            P("col", "row", None, None),
            P("col", "row", None),
            P(),
            P(),
        ),
        out_specs=P(None, "row", "col"),
        check_vma=False,
    )
```
